256 devices in a mesh: dp: 16 (over y, x), expert: 16 (over z, core).
Axes of the slice: x: 4, y: 4, z: 8, core: 2. Of those that a mesh axis runs over, the one named last changes fastest.
Arguments:
- tokens: bfloat16 [32768, 1024], P(('dp', 'expert')), may hold values from -24 to 24
- routes: int32 [32768, 8], P(('dp', 'expert')), may hold values from 0 to 63, all different within a row; in each aligned block of 128 rows (0 to 127, 128 to 255, ...) at most 24 rows name the same one
- gate_weights: float32 [32768, 8], P(('dp', 'expert')), may hold values from 0.05 to 0.25
- cotangent: bfloat16 [32768, 1024], P(('dp', 'expert')), may hold values from -24 to 24
- w_gate_up: bfloat16 [1024, 64, 768], P(None, 'expert'), may hold values from -0.1875 to 0.1875
- w_down: bfloat16 [1024, 64, 384], P(None, 'expert'), may hold values from -0.3125 to 0.3125
Outputs:
- layer_out: bfloat16 [32768, 1024], P(('dp', 'expert'))
- grad_tokens: bfloat16 [32768, 1024], P(('dp', 'expert'))
- grad_gate_up: bfloat16 [1024, 64, 768], P('dp', 'expert')
- grad_down: bfloat16 [1024, 64, 384], P('dp', 'expert')
The draws below stay inside these ranges and needn't reach their ends.
Inputs may be any that keep to these rules, and one draw needn't show every extreme that they name: `routes`: each row names 8 different experts. Among the 128 rows of one device no expert is named more than 24 times, and in some device's rows an expert is named exactly 24 times.
All inputs are finite; a program needn't handle non-finite values.
Results may differ from the reference program's by a relative error of at most 0.015.
Values may be sent and summed in bfloat16 or wider, within the bound.
A program may use at most 128 MiB of HBM per device.

```python
import math
import jax
import jax.numpy as jnp
import numpy as np
from jax import lax

D = 1024
H = 384
TOP = 8
TOK_DEV = 128
EXPERTS = 64
TOKENS = 32768
MOST = 24
N_DP = 16
N_EXPERT = 16


def spiked(array, own_key, source, target, blocks, factor):
    def block_of(dim):
        return (jnp.arange(array.shape[dim]) // (array.shape[dim] // blocks)).reshape((-1,) + (1,) * (array.ndim - 1 - dim))

    one_side = jax.random.permutation(own_key, blocks)[block_of(target)]
    far = (block_of(target) + blocks // 2) % blocks
    return jnp.where((block_of(source) == one_side) | (block_of(source) == far), factor * array, array)


def block_scale(rng, shape, pieces, least, top_value):
    level, own = 1.0, jax.random.fold_in(rng, 6)
    for dim, blocks in pieces:
        draws = jnp.exp(jax.random.uniform(jax.random.fold_in(own, dim), (blocks,), jnp.float32, least / len(pieces), top_value / len(pieces)))
        level = level * jnp.repeat(draws, shape[dim] // blocks).reshape([-1 if axis == dim else 1 for axis in range(len(shape))])
    return level


def routed_block(rng, own, number, rows, amount, top, limit, skew):
    ranking = jax.random.permutation(rng, amount)
    heavy_load, usual = shares(amount, rows * top, limit, skew, True), shares(amount, rows * top, limit, skew, False)
    places = jnp.arange(amount)

    def named(sizes, turn):
        used = int((sizes > 0).sum())
        fixed = max(1, used // 4)
        passed = fixed + (places - fixed + turn * (used - fixed)) % max(1, amount - fixed)
        return jnp.zeros((amount,), jnp.int32).at[ranking[jnp.where(places < fixed, places, passed)]].set(jnp.asarray(sizes, jnp.int32))

    sizes = jnp.where(number % 4 == 0, named(heavy_load, number // 4), named(usual, number - number // 4 - 1))
    mixed = jax.random.permutation(jax.random.fold_in(own, 3), amount)
    giver, taker = mixed[0:amount // 2 * 2:2], mixed[1:amount // 2 * 2:2]
    slack = jnp.minimum(sizes[giver] - 1, limit - sizes[taker]) // 2
    slack = jnp.where((giver == ranking[0]) | (taker == ranking[0]) | (sizes[taker] == 0), 0, jnp.maximum(slack, 0))
    passed = jax.random.randint(jax.random.fold_in(own, 4), (amount // 2,), 0, 1 << 20) % (slack + 1)
    sizes = sizes.at[giver].add(-passed).at[taker].add(passed)
    items = jnp.searchsorted(jnp.cumsum(sizes), jnp.arange(rows * top), side="right").astype(jnp.int32)
    listing = items.reshape(top, rows).T
    listing = listing[jax.random.permutation(jax.random.fold_in(own, 1), rows)]
    turn = jax.random.randint(jax.random.fold_in(own, 2), (rows, 1), 0, top)
    return jnp.take_along_axis(listing, (jnp.arange(top)[None, :] + turn) % top, axis=1)


def shares(amount, total, most, lean, full):
    weights = [(1 << 20) // math.isqrt(rank ** lean) + 1 for rank in range(1, amount + 1)]
    largest = most if full else min(most, max(-(-total // amount), total * weights[0] // sum(weights)))
    least = 1 if total - largest >= amount - 1 else 0
    counts, spare = [largest] + [least] * (amount - 1), total - largest - least * (amount - 1)
    while spare > 0:
        candidates = [i for i in range(1, amount) if counts[i] < largest] or [i for i in range(1, amount) if counts[i] < most]
        whole, budget = sum([weights[i] for i in candidates]), spare
        for i in candidates:
            extra = min(most - counts[i], max(1, budget * weights[i] // whole), spare)
            counts[i] = counts[i] + extra
            spare = spare - extra
    return np.array(counts)


def bell_draw(key, extent, spread, most, pieces=(), kind=jnp.bfloat16):
    values = spread * jax.random.normal(key, extent, jnp.float32)
    if pieces:
        values = values * block_scale(key, extent, pieces, -0.22, 0.18)
    return jnp.clip(values, -most, most).astype(kind)


def heavy_noise(own_key, extent, deviation, reach, cuts, heavy, kind=jnp.bfloat16):
    entries = deviation * jax.random.normal(own_key, extent, jnp.float32)
    if cuts:
        entries = entries * block_scale(own_key, extent, cuts, -0.22, 0.18)
    return jnp.clip(spiked(entries, jax.random.fold_in(own_key, 3), *heavy), -reach, reach).astype(kind)


def setup_inputs(seed: int = 0) -> dict:
    seeds = jax.random.split(jax.random.key(seed), 7)
    tokens = heavy_noise(seeds[0], (TOKENS, D), 1.0, 24.0, ((0, 256),), (0, 1, 256, 6.0))
    routes_keys = jax.random.split(jax.random.fold_in(seeds[1], 1), TOKENS // TOK_DEV)
    routes_turns = jax.random.permutation(jax.random.fold_in(seeds[1], 3), TOKENS // TOK_DEV)
    routes = jax.vmap(lambda own, number: routed_block(jax.random.fold_in(seeds[1], 2), own, number, TOK_DEV, EXPERTS, TOP, MOST, 2))(routes_keys, routes_turns).reshape((TOKENS, TOP))
    gate_weights = jnp.clip(0.05 + 0.2 * jax.random.uniform(seeds[2], (TOKENS, TOP), jnp.float32) ** block_scale(seeds[2], (TOKENS, TOP), ((0, 256),), -0.2, 0.2), 0.05, 0.25)
    cotangent = heavy_noise(seeds[3], (TOKENS, D), 1.0, 24.0, ((0, 256),), (0, 1, 256, 6.0))
    w_gate_up = bell_draw(seeds[4], (D, EXPERTS, 2 * H), D ** -0.5, 0.1875, ((1, 16),))
    w_down = bell_draw(seeds[5], (D, EXPERTS, H), H ** -0.5, 0.3125, ((1, 16),))
    return dict(tokens=tokens, routes=routes, gate_weights=gate_weights, cotangent=cotangent, w_gate_up=w_gate_up, w_down=w_down)


def split_parts(projected, hidden_units):
    gate_part = projected[..., :hidden_units]
    up_part = projected[..., hidden_units:]
    sigma = jax.nn.sigmoid(gate_part)
    return gate_part, up_part, sigma


def reference(tokens, routes, gate_weights, cotangent, w_gate_up, w_down):
    group_rows = TOK_DEV * N_EXPERT
    capacity = N_EXPERT * MOST
    assigned = group_rows * TOP
    slots_all = EXPERTS * capacity
    weights_gu = w_gate_up.astype(jnp.float32)
    weights_dn = w_down.astype(jnp.float32)

    def one_group(carry, operands):
        x_rows, route_rows, gate_rows, cot_rows = operands
        flat_routes = route_rows.reshape(assigned).astype(jnp.int32)
        onehot = (flat_routes[:, None] == jnp.arange(EXPERTS, dtype=jnp.int32)[None, :]).astype(jnp.int32)
        slot_rank = jnp.sum((jnp.cumsum(onehot, axis=0) - 1) * onehot, axis=1).astype(jnp.int32)
        slot_index = (flat_routes * capacity + slot_rank).astype(jnp.int32)
        source_of = jnp.zeros((slots_all,), jnp.int32).at[slot_index].set(jnp.arange(assigned, dtype=jnp.int32))
        filled = jnp.zeros((slots_all,), jnp.int32).at[slot_index].set(1) > 0
        token_of = (source_of // TOP).astype(jnp.int32)
        x_slots = jnp.where(filled[:, None], x_rows[token_of], 0).reshape(EXPERTS, capacity, D)
        projected = jnp.einsum('ecd,def->ecf', x_slots.astype(jnp.float32), weights_gu)
        gate_part, up_part, sigma = split_parts(projected, H)
        hidden = (gate_part * sigma * up_part).astype(jnp.bfloat16)
        expert_out = jnp.einsum('ech,deh->ecd', hidden.astype(jnp.float32), weights_dn).astype(jnp.bfloat16)
        per_assign = expert_out.reshape(slots_all, D)[slot_index].astype(jnp.float32).reshape(group_rows, TOP, D)
        layer_out = jnp.sum(per_assign * gate_rows[:, :, None], axis=1).astype(jnp.bfloat16)
        weighted = (gate_rows[:, :, None] * cot_rows.astype(jnp.float32)[:, None, :]).astype(jnp.bfloat16)
        weighted = weighted.reshape(assigned, D)
        cot_slots = jnp.where(filled[:, None], weighted[source_of], 0).reshape(EXPERTS, capacity, D)
        d_hidden = jnp.einsum('ecd,deh->ech', cot_slots.astype(jnp.float32), weights_dn)
        d_gate = d_hidden * up_part * sigma * (1.0 + gate_part * (1.0 - sigma))
        d_up = d_hidden * gate_part * sigma
        d_proj = jnp.concatenate([d_gate, d_up], axis=-1).astype(jnp.bfloat16)
        slot_grads = jnp.einsum('ecf,def->ecd', d_proj.astype(jnp.float32), weights_gu).astype(jnp.bfloat16)
        grad_assign = slot_grads.reshape(slots_all, D)[slot_index].astype(jnp.float32).reshape(group_rows, TOP, D)
        grad_rows = jnp.sum(grad_assign, axis=1).astype(jnp.bfloat16)
        part_gu = jnp.einsum('ecd,ecf->def', x_slots.astype(jnp.float32), d_proj.astype(jnp.float32)).astype(jnp.bfloat16)
        part_dn = jnp.einsum('ecd,ech->deh', cot_slots.astype(jnp.float32), hidden.astype(jnp.float32)).astype(jnp.bfloat16)
        summed_gu, summed_dn = carry
        carry = (summed_gu + part_gu.astype(jnp.float32), summed_dn + part_dn.astype(jnp.float32))
        return carry, (layer_out, grad_rows)

    start_carry = (jnp.zeros((D, EXPERTS, 2 * H), jnp.float32), jnp.zeros((D, EXPERTS, H), jnp.float32))
    operands = (tokens.reshape(N_DP, group_rows, D), routes.reshape(N_DP, group_rows, TOP),
                gate_weights.reshape(N_DP, group_rows, TOP), cotangent.reshape(N_DP, group_rows, D))
    totals, stacked = lax.scan(one_group, start_carry, operands)
    layer_out = stacked[0].reshape(TOKENS, D)
    grad_tokens = stacked[1].reshape(TOKENS, D)
    return layer_out, grad_tokens, totals[0].astype(jnp.bfloat16), totals[1].astype(jnp.bfloat16)
```

```python
import jax
import jax.numpy as jnp
from jax import lax
from jax.experimental import pallas as pl
from jax.experimental.pallas import tpu as pltpu
from jax.sharding import PartitionSpec as P

MESH = pl.DeviceIdType.MESH
F32 = jnp.float32
BF16 = jnp.bfloat16

NZ = 8
NX = 4
TOK = 128
D = 1024
H = 384
F = 2 * H
W3 = 3 * H
L = 4
MOST = 24
PAIR = 2 * MOST
ROWS = L * PAIR
SLOTS = NZ * PAIR


def place(distance):
    return (distance + 2) % NZ


def dot(a, b, dims):
    return lax.dot_general(a, b, ((dims[:1], dims[1:]), ((), ())), preferred_element_type=F32)


def kernel(
    x_ref, rt_ref, gt_ref, c_ref, wgu_hbm, wdn_hbm,
    lo_ref, go_ref, ogu_ref, odn_ref,
    W, rawg, rawd, xg, cg, mg, Xs, Cs, GH, DP, Gs, Pm, OR, GR,
    sibo, sibg, rlp, rgp, rlm, rgm,
    fwd1, fin1, fwd2, fin2, fs,
    ring_s, ring_r, sib_s, sib_r, rsib_s, rsib_r, rz_s, rz_r, x1_s, x1_r, x2_s, x2_r, raw_sem,
):
    dp, ex = lax.axis_index("dp"), lax.axis_index("expert")
    yy, xx = dp // NX, dp % NX
    zz, core = ex // 2, ex % 2

    def at_z(step):
        return (dp, ((zz + step) % NZ) * 2 + core)

    def at_x(step):
        return (yy * NX + (xx + step) % NX, ex)

    def at_y(step):
        return (((yy + step) % NX) * NX + xx, ex)

    zp, zm, sib = at_z(1), at_z(NZ - 1), (dp, zz * 2 + 1 - core)
    xp, xm, yp, ym = at_x(1), at_x(NX - 1), at_y(1), at_y(NX - 1)

    def raw_copies(group):
        rows = pl.ds(group * 256, 256)
        return (
            pltpu.make_async_copy(wgu_hbm.at[rows], rawg, raw_sem.at[0]),
            pltpu.make_async_copy(wdn_hbm.at[rows], rawd, raw_sem.at[1]),
        )

    for copy in raw_copies(0):
        copy.start()

    mg[place(0), 0, 0:8, :] = rt_ref[...].astype(F32)
    mg[place(0), 0, 8:16, :] = gt_ref[...]

    barrier = pltpu.get_barrier_semaphore()
    for peer in (zp, zm, sib, xp, xm, yp, ym):
        pl.semaphore_signal(barrier, inc=1, device_id=peer, device_id_type=MESH)
    pl.semaphore_wait(barrier, 7)

    sends = []

    def send(src, dst, send_sem, recv_sem, peer):
        copy = pltpu.make_async_remote_copy(
            src_ref=src, dst_ref=dst, send_sem=send_sem, recv_sem=recv_sem,
            device_id=peer, device_id_type=MESH,
        )
        copy.start()
        sends.append(copy)

    def arrived(dst, recv_sem):
        pltpu.make_async_remote_copy(
            src_ref=dst, dst_ref=dst, send_sem=recv_sem, recv_sem=recv_sem,
            device_id=zp, device_id_type=MESH,
        ).wait_recv()

    def block(t, distance, column):
        if t == 2:
            return mg.at[place(distance), column]
        return (xg, cg)[t].at[place(distance), pl.ds(column * TOK, TOK)]

    far = {0: (4, 3), 1: (3, 4), 2: (4, 3)}
    own = {0: x_ref, 1: c_ref, 2: mg.at[place(0), 0]}
    for t in (2, 0, 1):
        send(own[t], block(t, NZ - 1, 0), ring_s.at[t, 0, 0], ring_r.at[t, NZ - 1], zp)
        send(own[t], block(t, 1, 0), ring_s.at[t, 1, 0], ring_r.at[t, 1], zm)
        send(own[t], block(t, 0, 1), sib_s.at[t, 0], sib_r.at[t, 0], sib)
    xg[place(0), 0:TOK] = x_ref[...]
    cg[place(0), 0:TOK] = c_ref[...]

    def hop(k, tensors):
        for t in tensors:
            for way, distance, peer, further in ((0, NZ - k, zp, NZ - k - 1), (1, k, zm, k + 1)):
                if k > far[t][way]:
                    continue
                arrived(block(t, distance, 0), ring_r.at[t, distance])
                if k < far[t][way]:
                    send(block(t, distance, 0), block(t, further, 0), ring_s.at[t, way, k], ring_r.at[t, further], peer)
                send(block(t, distance, 0), block(t, distance, 1), sib_s.at[t, distance], sib_r.at[t, distance], sib)

    def relayout(group):
        for copy in raw_copies(group):
            copy.wait()

        def body(i, carry):
            rows = pl.ds(i * 64, 64)
            W[:, group, i, :, 0:F] = jnp.swapaxes(rawg[rows], 0, 1)
            W[:, group, i, :, F:W3] = jnp.swapaxes(rawd[rows], 0, 1)
            return carry

        lax.fori_loop(0, NX, body, 0)
        if group < NX - 1:
            for copy in raw_copies(group + 1):
                copy.start()

    def dispatch(distance):
        for t in (2, 0, 1):
            arrived(block(t, distance, 1), sib_r.at[t, distance])
        i = place(distance)
        first = (ex * L).astype(F32)
        earlier = (
            lax.broadcasted_iota(jnp.int32, (TOK, TOK), 0) < lax.broadcasted_iota(jnp.int32, (TOK, TOK), 1)
        ).astype(BF16)
        slot = lax.broadcasted_iota(jnp.int32, (MOST, TOK), 0).astype(F32)
        sub = lax.broadcasted_iota(jnp.int32, (8, TOK), 0)
        empty = jnp.zeros((MOST, TOK), F32)
        pieces = [[None, None] for _ in range(L)]
        for c in range(2):
            named, gates = mg[i, c, 0:8, :], mg[i, c, 8:16, :]
            masks, weights = [], []
            stacked = jnp.zeros((8, TOK), F32)
            for l in range(L):
                hit = named == first + l
                mask = jnp.sum(hit.astype(F32), axis=0, keepdims=True)
                masks.append(mask)
                weights.append(jnp.sum(jnp.where(hit, gates, 0.0), axis=0, keepdims=True))
                stacked = jnp.where(sub == l, mask, stacked)
            rank = dot(stacked.astype(BF16), earlier, (1, 0))
            for l in range(L):
                chosen = jnp.where((slot == rank[l : l + 1]) & (masks[l] > 0.0), 1.0, 0.0)
                gate = jnp.sum(chosen * weights[l], axis=1, keepdims=True)
                Gs[l, i * PAIR + c * MOST : i * PAIR + (c + 1) * MOST, :] = jnp.broadcast_to(gate, (MOST, TOK))
                pieces[l][c] = jnp.concatenate([chosen, empty] if c == 0 else [empty, chosen], axis=1)
        picked = jnp.concatenate([pieces[l][c] for l in range(L) for c in range(2)], axis=0).astype(BF16)
        Pm[i] = picked
        for gathered, slots in ((xg, Xs), (cg, Cs)):
            got = dot(picked, gathered[i], (1, 0)).astype(BF16)
            for l in range(L):
                slots[l, i * PAIR : (i + 1) * PAIR, :] = got[l * PAIR : (l + 1) * PAIR]

    def experts(i0, i1):
        r0, r1 = i0 * PAIR, i1 * PAIR

        def body(l, carry):
            up_w = W[l, :, :, :, 0:F].reshape(D, F)
            down_w = W[l, :, :, :, F:W3].reshape(D, H)
            gate = Gs[l, r0:r1, 0:1]
            projected = dot(Xs[l, r0:r1], up_w, (1, 0))
            g, u = projected[:, :H], projected[:, H:]
            s = jax.nn.sigmoid(g)
            gs = g * s
            hidden = (gs * u * gate).astype(BF16)
            GH[l, r0:r1] = hidden
            d_hidden = dot(Cs[l, r0:r1], down_w, (1, 0)) * gate
            d_gate = d_hidden * u * s * (1.0 + g * (1.0 - s))
            d_proj = jnp.concatenate([d_gate, d_hidden * gs], axis=1).astype(BF16)
            DP[l, r0:r1] = d_proj
            out = dot(hidden, down_w, (1, 1)).astype(BF16)
            back = dot(d_proj, up_w, (1, 1)).astype(BF16)
            at = pl.ds(pl.multiple_of(l * PAIR, 16), PAIR)
            for i in range(i0, i1):
                part = slice((i - i0) * PAIR, (i - i0 + 1) * PAIR)
                OR[i, at, :] = out[part]
                GR[i, at, :] = back[part]
            return carry

        lax.fori_loop(0, L, body, 0)

    relayout(0)
    relayout(1)
    hop(1, (2, 0))
    relayout(2)
    dispatch(0)
    hop(1, (1,))
    relayout(3)
    dispatch(1)
    dispatch(NZ - 1)
    hop(2, (2, 0))
    hop(2, (1,))
    dispatch(2)
    dispatch(NZ - 2)
    hop(3, (2, 0))
    experts(0, 5)
    hop(3, (1,))
    dispatch(3)
    dispatch(NZ - 3)
    hop(4, (2, 0, 1))
    dispatch(4)
    experts(5, 8)
    for copy in sends:
        copy.wait_send()
    sends.clear()

    def gradients(l0, l1):
        def body(n, carry):
            l, q = l0 + n // NX, n % NX
            columns = pl.ds(pl.multiple_of(q * 256, 256), 256)
            W[l, q, :, :, 0:F] = dot(Xs[l, :, columns], DP[l], (0, 0)).astype(BF16).reshape(NX, 64, F)
            W[l, q, :, :, F:W3] = dot(Cs[l, :, columns], GH[l], (0, 0)).astype(BF16).reshape(NX, 64, H)
            return carry

        lax.fori_loop(0, (l1 - l0) * NX, body, 0)

    def piece1(h, l, q):
        return W.at[l, :, q] if h == 0 else W.at[l, q]

    def piece2(h, l, q):
        return W.at[l, q, xx] if h == 0 else W.at[l, yy, q]

    def axes(h, stage):
        along_x = (h == 0) == (stage == 1)
        return (xx, xp, xm) if along_x else (yy, yp, ym)

    def spread(stage, h):
        at, plus, minus = axes(h, stage)
        piece, fwd, fin, s, r = (
            (piece1, fwd1, fin1, x1_s, x1_r) if stage == 1 else (piece2, fwd2, fin2, x2_s, x2_r)
        )
        la, lb = 2 * h, 2 * h + 1
        send(piece(h, la, (at + 2) % NX), fwd.at[h, 0], s.at[h, 0, 0], r.at[h, 0, 0], plus)
        send(piece(h, lb, (at + 2) % NX), fwd.at[h, 1], s.at[h, 1, 0], r.at[h, 1, 0], minus)
        send(piece(h, lb, (at + 1) % NX), fin.at[h, 0, 1], s.at[h, 0, 1], r.at[h, 0, 1], plus)
        send(piece(h, la, (at + 3) % NX), fin.at[h, 1, 0], s.at[h, 1, 1], r.at[h, 1, 1], minus)

    def relay(stage, h):
        at, plus, minus = axes(h, stage)
        fwd, fin, s, r = (fwd1, fin1, x1_s, x1_r) if stage == 1 else (fwd2, fin2, x2_s, x2_r)
        for way, l, q, peer, slot in ((0, 2 * h, (at + 1) % NX, plus, 0), (1, 2 * h + 1, (at + 3) % NX, minus, 1)):
            arrived(fwd.at[h, way], r.at[h, way, 0])
            if stage == 1:

                def body(n, carry):
                    mine = W[l, n, q] if h == 0 else W[l, q, n]
                    fwd1[h, way, n] = (fwd1[h, way, n].astype(F32) + mine.astype(F32)).astype(BF16)
                    return carry

                lax.fori_loop(0, NX, body, 0)
            else:
                mine = W[l, q, xx] if h == 0 else W[l, yy, q]
                fwd2[h, way] = (fwd2[h, way].astype(F32) + mine.astype(F32)).astype(BF16)
            send(fwd.at[h, way], fin.at[h, way, slot], s.at[h, way, 2], r.at[h, way, 2], peer)

    def settle(stage, h):
        at, plus, minus = axes(h, stage)
        fin, r = (fin1, x1_r) if stage == 1 else (fin2, x2_r)
        for way, slot, n in ((0, 1, 1), (1, 0, 1), (0, 0, 2), (1, 1, 2)):
            arrived(fin.at[h, way, slot], r.at[h, way, n])
        for slot in range(2):
            l = 2 * h + slot
            if stage == 1:

                def body(n, carry):
                    a, b = (n, at) if h == 0 else (at, n)
                    total = W[l, a, b].astype(F32) + fin1[h, 0, slot, n].astype(F32) + fin1[h, 1, slot, n].astype(F32)
                    W[l, a, b] = total.astype(BF16)
                    return carry

                lax.fori_loop(0, NX, body, 0)
            else:
                total = W[l, yy, xx].astype(F32) + fin2[h, 0, slot].astype(F32) + fin2[h, 1, slot].astype(F32)
                fs[l] = total.astype(BF16)

    def combine(i0, i1):
        def body(i, carry):
            picked = Pm[i]
            xg[i] = dot(picked, OR[i], (0, 0)).astype(BF16)
            cg[i] = dot(picked, GR[i], (0, 0)).astype(BF16)
            return carry

        lax.fori_loop(i0, i1, body, 0)
        for i in range(i0, i1):
            send(xg.at[i, pl.ds(TOK, TOK)], sibo.at[i], rsib_s.at[0, i], rsib_r.at[0, i], sib)
            send(cg.at[i, pl.ds(TOK, TOK)], sibg.at[i], rsib_s.at[1, i], rsib_r.at[1, i], sib)

    def total_of(parts):
        total = parts[0].astype(F32)
        for part in parts[1:]:
            total = total + part.astype(F32)
        return total.astype(BF16)

    ways = (
        (0, 0, (4, 3, 2, 1), rlp, zp),
        (1, 1, (4, 5, 6, 7), rgm, zm),
        (1, 0, (3, 2, 1), rgp, zp),
        (0, 1, (5, 6, 7), rlm, zm),
    )

    def reduce_step(j):
        for t, way, targets, slots, peer in ways:
            if j >= len(targets):
                continue
            i = place(targets[j])
            mine, other = ((xg, sibo), (cg, sibg))[t]
            arrived(other.at[i], rsib_r.at[t, i])
            if j > 0:
                arrived(slots.at[j - 1], rz_r.at[t, way, j - 1])

            def body(n, carry):
                rows = pl.ds(pl.multiple_of(n * 32, 32), 32)
                parts = [mine[i, rows, :], other[i, rows, :]]
                if j > 0:
                    parts.append(slots[j - 1, rows, :])
                mine[i, rows, :] = total_of(parts)
                return carry

            lax.fori_loop(0, TOK // 32, body, 0)
            send(mine.at[i, pl.ds(0, TOK)], slots.at[j], rz_s.at[t, way, j], rz_r.at[t, way, j], peer)

    def reduce_end():
        i = place(0)
        for t, mine, other, plus, minus, out in ((0, xg, sibo, rlp, rlm, lo_ref), (1, cg, sibg, rgp, rgm, go_ref)):
            np_, nm = (3, 2) if t == 0 else (2, 3)
            arrived(other.at[i], rsib_r.at[t, i])
            arrived(plus.at[np_], rz_r.at[t, 0, np_])
            arrived(minus.at[nm], rz_r.at[t, 1, nm])

            def body(n, carry):
                rows = pl.ds(pl.multiple_of(n * 32, 32), 32)
                out[rows, :] = total_of([mine[i, rows, :], other[i, rows, :], plus[np_, rows, :], minus[nm, rows, :]])
                return carry

            lax.fori_loop(0, TOK // 32, body, 0)

    gradients(0, 2)
    spread(1, 0)
    combine(5, 8)
    gradients(2, 4)
    spread(1, 1)
    reduce_step(0)
    combine(0, 5)
    relay(1, 0)
    relay(1, 1)
    reduce_step(1)
    reduce_step(2)
    reduce_step(3)
    settle(1, 0)
    spread(2, 0)
    settle(1, 1)
    spread(2, 1)
    relay(2, 0)
    relay(2, 1)
    reduce_end()
    settle(2, 0)
    settle(2, 1)
    ogu_ref[...] = jnp.swapaxes(fs[:, :, 0:F], 0, 1)
    odn_ref[...] = jnp.swapaxes(fs[:, :, F:W3], 0, 1)
    for copy in sends:
        copy.wait_send()


def per_device(tokens, routes, gate_weights, cotangent, w_gate_up, w_down):
    vmem = pl.BlockSpec(memory_space=pltpu.VMEM)
    hbm = pl.BlockSpec(memory_space=pl.ANY)
    dma = pltpu.SemaphoreType.DMA
    rows = D // (NX * NX)
    return pl.pallas_call(
        kernel,
        out_shape=(
            jax.ShapeDtypeStruct((TOK, D), BF16),
            jax.ShapeDtypeStruct((TOK, D), BF16),
            jax.ShapeDtypeStruct((rows, L, F), BF16),
            jax.ShapeDtypeStruct((rows, L, H), BF16),
        ),
        in_specs=[vmem, vmem, vmem, vmem, hbm, hbm],
        out_specs=(vmem, vmem, vmem, vmem),
        scratch_shapes=[
            pltpu.VMEM((L, NX, NX, rows, W3), BF16),
            pltpu.VMEM((256, L, F), BF16),
            pltpu.VMEM((256, L, H), BF16),
            pltpu.VMEM((NZ, 2 * TOK, D), BF16),
            pltpu.VMEM((NZ, 2 * TOK, D), BF16),
            pltpu.VMEM((NZ, 2, 16, TOK), F32),
            pltpu.VMEM((L, SLOTS, D), BF16),
            pltpu.VMEM((L, SLOTS, D), BF16),
            pltpu.VMEM((L, SLOTS, H), BF16),
            pltpu.VMEM((L, SLOTS, F), BF16),
            pltpu.VMEM((L, SLOTS, TOK), F32),
            pltpu.VMEM((NZ, ROWS, 2 * TOK), BF16),
            pltpu.VMEM((NZ, ROWS, D), BF16),
            pltpu.VMEM((NZ, ROWS, D), BF16),
            pltpu.VMEM((NZ, TOK, D), BF16),
            pltpu.VMEM((NZ, TOK, D), BF16),
            pltpu.VMEM((4, TOK, D), BF16),
            pltpu.VMEM((3, TOK, D), BF16),
            pltpu.VMEM((3, TOK, D), BF16),
            pltpu.VMEM((4, TOK, D), BF16),
            pltpu.VMEM((2, 2, NX, rows, W3), BF16),
            pltpu.VMEM((2, 2, 2, NX, rows, W3), BF16),
            pltpu.VMEM((2, 2, rows, W3), BF16),
            pltpu.VMEM((2, 2, 2, rows, W3), BF16),
            pltpu.VMEM((L, rows, W3), BF16),
            dma((3, 2, 4)), dma((3, NZ)), dma((3, NZ)), dma((3, NZ)),
            dma((2, NZ)), dma((2, NZ)), dma((2, 2, 4)), dma((2, 2, 4)),
            dma((2, 2, 3)), dma((2, 2, 3)), dma((2, 2, 3)), dma((2, 2, 3)),
            dma((2,)),
        ],
        compiler_params=pltpu.CompilerParams(
            collective_id=0, has_side_effects=True, vmem_limit_bytes=63 << 20
        ),
    )(tokens, routes.T, gate_weights.T, cotangent, w_gate_up, w_down)


def solution(mesh):
    rows = P(("dp", "expert"), None)
    return jax.shard_map(
        per_device,
        mesh=mesh,
        in_specs=(rows, rows, rows, rows, P(None, "expert", None), P(None, "expert", None)),
        out_specs=(rows, rows, P("dp", "expert", None), P("dp", "expert", None)),
        check_vma=False,
    )
```

```python
import jax
import jax.numpy as jnp
from jax import lax
from jax.experimental import pallas as pl
from jax.experimental.pallas import tpu as pltpu
from jax.sharding import PartitionSpec as P

MESH = pl.DeviceIdType.MESH
F32 = jnp.float32
BF16 = jnp.bfloat16

NZ = 8
NX = 4
TOK = 128
D = 1024
H = 384
F = 2 * H
W3 = 3 * H
L = 4
MOST = 24
PAIR = 2 * MOST
ROWS = L * PAIR
SLOTS = NZ * PAIR


ORDER = (0, 1, 7, 2, 6, 3, 5, 4)


def place(distance):
    return ORDER.index(distance)


def dot(a, b, dims):
    return lax.dot_general(a, b, ((dims[:1], dims[1:]), ((), ())), preferred_element_type=F32)


def kernel(
    x_hbm, rt_ref, gt_ref, c_hbm, wgu_hbm, wdn_hbm,
    lo_ref, go_ref, ogu_ref, odn_ref,
    W, rawg, rawd, xg, cg, mg, Xs, Cs, GH, DP, Gs, Pm, OR, GR,
    sibo, sibg, rlp, rgp, rlm, rgm,
    fwd1, fin1, fwd2, fin2, fs,
    ring_s, ring_r, sib_s, sib_r, rsib_s, rsib_r, rz_s, rz_r, x1_s, x1_r, x2_s, x2_r, raw_sem, own_sem,
):
    dp, ex = lax.axis_index("dp"), lax.axis_index("expert")
    yy, xx = dp // NX, dp % NX
    zz, core = ex // 2, ex % 2

    def at_z(step):
        return (dp, ((zz + step) % NZ) * 2 + core)

    def at_x(step):
        return (yy * NX + (xx + step) % NX, ex)

    def at_y(step):
        return (((yy + step) % NX) * NX + xx, ex)

    zp, zm, sib = at_z(1), at_z(NZ - 1), (dp, zz * 2 + 1 - core)
    xp, xm, yp, ym = at_x(1), at_x(NX - 1), at_y(1), at_y(NX - 1)

    def raw_copies(group):
        rows = pl.ds(group * 256, 256)
        return (
            pltpu.make_async_copy(wgu_hbm.at[rows], rawg, raw_sem.at[0]),
            pltpu.make_async_copy(wdn_hbm.at[rows], rawd, raw_sem.at[1]),
        )

    own_copies = [
        pltpu.make_async_copy(source, gathered.at[place(0), pl.ds(0, TOK)], own_sem.at[n])
        for n, (source, gathered) in enumerate(((x_hbm, xg), (c_hbm, cg)))
    ]
    for copy in own_copies + list(raw_copies(0)):
        copy.start()

    mg[place(0), 0, 0:8, :] = rt_ref[...].astype(F32)
    mg[place(0), 0, 8:16, :] = gt_ref[...]

    barrier = pltpu.get_barrier_semaphore()
    for peer in (zp, zm, sib, xp, xm, yp, ym):
        pl.semaphore_signal(barrier, inc=1, device_id=peer, device_id_type=MESH)
    pl.semaphore_wait(barrier, 7)

    sends, reading = [], {}

    def send(src, dst, send_sem, recv_sem, peer, source_place=None):
        copy = pltpu.make_async_remote_copy(
            src_ref=src, dst_ref=dst, send_sem=send_sem, recv_sem=recv_sem,
            device_id=peer, device_id_type=MESH,
        )
        copy.start()
        (sends if source_place is None else reading.setdefault(source_place, [])).append(copy)

    def arrived(dst, recv_sem):
        pltpu.make_async_remote_copy(
            src_ref=dst, dst_ref=dst, send_sem=recv_sem, recv_sem=recv_sem,
            device_id=zp, device_id_type=MESH,
        ).wait_recv()

    def block(t, distance, column):
        if t == 2:
            return mg.at[place(distance), column]
        return (xg, cg)[t].at[place(distance), pl.ds(column * TOK, TOK)]

    far = {0: (4, 3), 1: (3, 4), 2: (4, 3)}
    own = {0: x_hbm, 1: c_hbm, 2: mg.at[place(0), 0]}
    for t in (2, 0, 1):
        send(own[t], block(t, NZ - 1, 0), ring_s.at[t, 0, 0], ring_r.at[t, NZ - 1], zp)
        send(own[t], block(t, 1, 0), ring_s.at[t, 1, 0], ring_r.at[t, 1], zm)
        send(own[t], block(t, 0, 1), sib_s.at[t, 0], sib_r.at[t, 0], sib)

    def hop(k, tensors):
        for t in tensors:
            for way, distance, peer, further in ((0, NZ - k, zp, NZ - k - 1), (1, k, zm, k + 1)):
                if k > far[t][way]:
                    continue
                arrived(block(t, distance, 0), ring_r.at[t, distance])
                if k < far[t][way]:
                    send(block(t, distance, 0), block(t, further, 0), ring_s.at[t, way, k], ring_r.at[t, further], peer, place(distance))
                send(block(t, distance, 0), block(t, distance, 1), sib_s.at[t, distance], sib_r.at[t, distance], sib, place(distance))

    def relayout(group):
        for copy in raw_copies(group):
            copy.wait()

        def body(i, carry):
            rows = pl.ds(i * 64, 64)
            W[:, group, i, :, 0:F] = jnp.swapaxes(rawg[rows], 0, 1)
            W[:, group, i, :, F:W3] = jnp.swapaxes(rawd[rows], 0, 1)
            return carry

        lax.fori_loop(0, NX, body, 0)
        if group < NX - 1:
            for copy in raw_copies(group + 1):
                copy.start()

    def dispatch(distance):
        for t in (2, 0, 1):
            arrived(block(t, distance, 1), sib_r.at[t, distance])
        i = place(distance)
        first = (ex * L).astype(F32)
        earlier = (
            lax.broadcasted_iota(jnp.int32, (TOK, TOK), 0) < lax.broadcasted_iota(jnp.int32, (TOK, TOK), 1)
        ).astype(BF16)
        slot = lax.broadcasted_iota(jnp.int32, (MOST, TOK), 0).astype(F32)
        sub = lax.broadcasted_iota(jnp.int32, (8, TOK), 0)
        empty = jnp.zeros((MOST, TOK), F32)
        pieces = [[None, None] for _ in range(L)]
        for c in range(2):
            named, gates = mg[i, c, 0:8, :], mg[i, c, 8:16, :]
            masks, weights = [], []
            stacked = jnp.zeros((8, TOK), F32)
            for l in range(L):
                hit = named == first + l
                mask = jnp.sum(hit.astype(F32), axis=0, keepdims=True)
                masks.append(mask)
                weights.append(jnp.sum(jnp.where(hit, gates, 0.0), axis=0, keepdims=True))
                stacked = jnp.where(sub == l, mask, stacked)
            rank = dot(stacked.astype(BF16), earlier, (1, 0))
            for l in range(L):
                chosen = jnp.where((slot == rank[l : l + 1]) & (masks[l] > 0.0), 1.0, 0.0)
                gate = jnp.sum(chosen * weights[l], axis=1, keepdims=True)
                Gs[l, i * PAIR + c * MOST : i * PAIR + (c + 1) * MOST, :] = jnp.broadcast_to(gate, (MOST, TOK))
                pieces[l][c] = jnp.concatenate([chosen, empty] if c == 0 else [empty, chosen], axis=1)
        picked = jnp.concatenate([pieces[l][c] for l in range(L) for c in range(2)], axis=0).astype(BF16)
        Pm[i] = picked
        for gathered, slots in ((xg, Xs), (cg, Cs)):
            got = dot(picked, gathered[i], (1, 0)).astype(BF16)
            for l in range(L):
                slots[l, i * PAIR : (i + 1) * PAIR, :] = got[l * PAIR : (l + 1) * PAIR]

    def experts(i0, i1):
        r0, r1 = i0 * PAIR, i1 * PAIR

        def body(l, carry):
            up_w = W[l, :, :, :, 0:F].reshape(D, F)
            down_w = W[l, :, :, :, F:W3].reshape(D, H)
            gate = Gs[l, r0:r1, 0:1]
            projected = dot(Xs[l, r0:r1], up_w, (1, 0))
            g, u = projected[:, :H], projected[:, H:]
            s = jax.nn.sigmoid(g)
            gs = g * s
            hidden = (gs * u * gate).astype(BF16)
            GH[l, r0:r1] = hidden
            d_hidden = dot(Cs[l, r0:r1], down_w, (1, 0)) * gate
            d_gate = d_hidden * u * s * (1.0 + g * (1.0 - s))
            d_proj = jnp.concatenate([d_gate, d_hidden * gs], axis=1).astype(BF16)
            DP[l, r0:r1] = d_proj
            out = dot(hidden, down_w, (1, 1)).astype(BF16)
            back = dot(d_proj, up_w, (1, 1)).astype(BF16)
            at = pl.ds(pl.multiple_of(l * PAIR, 16), PAIR)
            for i in range(i0, i1):
                part = slice((i - i0) * PAIR, (i - i0 + 1) * PAIR)
                OR[i, at, :] = out[part]
                GR[i, at, :] = back[part]
            return carry

        lax.fori_loop(0, L, body, 0)

    def combine(i0, i1):
        def body(i, carry):
            picked = Pm[i]
            xg[i] = dot(picked, OR[i], (0, 0)).astype(BF16)
            cg[i] = dot(picked, GR[i], (0, 0)).astype(BF16)
            return carry

        for i in range(i0, i1):
            for copy in reading.pop(i, []):
                copy.wait_send()
        lax.fori_loop(i0, i1, body, 0)
        for i in range(i0, i1):
            send(xg.at[i, pl.ds(TOK, TOK)], sibo.at[i], rsib_s.at[0, i], rsib_r.at[0, i], sib)
            send(cg.at[i, pl.ds(TOK, TOK)], sibg.at[i], rsib_s.at[1, i], rsib_r.at[1, i], sib)

    for group in range(NX):
        relayout(group)
    for copy in own_copies:
        copy.wait()
    hop(1, (2, 0))
    hop(1, (1,))
    for distance in (0, 1, 7):
        dispatch(distance)
    experts(0, 3)
    hop(2, (2, 0))
    hop(2, (1,))
    dispatch(2)
    dispatch(6)
    experts(3, 5)
    combine(0, 3)
    hop(3, (2, 0))
    hop(3, (1,))
    dispatch(3)
    dispatch(5)
    experts(5, 7)
    combine(3, 5)
    hop(4, (2, 0, 1))
    dispatch(4)
    experts(7, 8)

    def gradient(l, q):
        columns = pl.ds(pl.multiple_of(q * 256, 256), 256)
        W[l, q, :, :, 0:F] = dot(Xs[l, :, columns], DP[l], (0, 0)).astype(BF16).reshape(NX, 64, F)
        W[l, q, :, :, F:W3] = dot(Cs[l, :, columns], GH[l], (0, 0)).astype(BF16).reshape(NX, 64, H)

    def chunk(h, l, q, n):
        return (l, n, q) if h == 0 else (l, q, n)

    def axes(h, stage):
        along_x = (h == 0) == (stage == 1)
        return (xx, xp, xm) if along_x else (yy, yp, ym)

    def second(h, o):
        return (axes(h, 2)[0] + o) % NX

    def far1(h, way, o):
        at, plus, minus = axes(h, 1)
        n = second(h, o)
        send(
            W.at[chunk(h, 2 * h + way, (at + 2) % NX, n)], fwd1.at[h, way, n],
            x1_s.at[h, way, o], x1_r.at[h, way, o], (plus, minus)[way],
        )

    def near1(h, way):
        at, plus, minus = axes(h, 1)
        l, q = 2 * h + 1 - way, (at + (1, 3)[way]) % NX
        source = W.at[l, :, q] if h == 0 else W.at[l, q]
        send(source, fin1.at[h, way, 1 - way], x1_s.at[h, way, 4], x1_r.at[h, way, 4], (plus, minus)[way])

    def relay1(h, way, o):
        at, plus, minus = axes(h, 1)
        n = second(h, o)
        arrived(fwd1.at[h, way, n], x1_r.at[h, way, o])
        mine = W[chunk(h, 2 * h + way, (at + (1, 3)[way]) % NX, n)]
        fwd1[h, way, n] = (fwd1[h, way, n].astype(F32) + mine.astype(F32)).astype(BF16)
        send(
            fwd1.at[h, way, n], fin1.at[h, way, way, n],
            x1_s.at[h, way, 5 + o], x1_r.at[h, way, 5 + o], (plus, minus)[way],
        )

    def settle1(h, o):
        at = axes(h, 1)[0]
        n = second(h, o)
        for way in range(2):
            if o == 2:
                arrived(fin1.at[h, way, 1 - way], x1_r.at[h, way, 4])
            arrived(fin1.at[h, way, way, n], x1_r.at[h, way, 5 + o])
        for slot in range(2):
            own = chunk(h, 2 * h + slot, at, n)
            total = W[own].astype(F32) + fin1[h, 0, slot, n].astype(F32) + fin1[h, 1, slot, n].astype(F32)
            W[own] = total.astype(BF16)

    def held(h, l, q):
        return chunk(h, l, axes(h, 1)[0], q)

    def far2(h):
        for way in range(2):
            send(
                W.at[held(h, 2 * h + way, second(h, 2))], fwd2.at[h, way],
                x2_s.at[h, way, 0], x2_r.at[h, way, 0], axes(h, 2)[1 + way],
            )

    def near2(h, way):
        send(
            W.at[held(h, 2 * h + 1 - way, second(h, (1, 3)[way]))], fin2.at[h, way, 1 - way],
            x2_s.at[h, way, 1], x2_r.at[h, way, 1], axes(h, 2)[1 + way],
        )

    def relay2(h, way):
        arrived(fwd2.at[h, way], x2_r.at[h, way, 0])
        mine = W[held(h, 2 * h + way, second(h, (1, 3)[way]))]
        fwd2[h, way] = (fwd2[h, way].astype(F32) + mine.astype(F32)).astype(BF16)
        send(fwd2.at[h, way], fin2.at[h, way, way], x2_s.at[h, way, 2], x2_r.at[h, way, 2], axes(h, 2)[1 + way])

    def settle2(h):
        for way in range(2):
            arrived(fin2.at[h, way, 1 - way], x2_r.at[h, way, 1])
            arrived(fin2.at[h, way, way], x2_r.at[h, way, 2])
        for slot in range(2):
            l = 2 * h + slot
            total = W[l, yy, xx].astype(F32) + fin2[h, 0, slot].astype(F32) + fin2[h, 1, slot].astype(F32)
            fs[l] = total.astype(BF16)

    def total_of(parts):
        total = parts[0].astype(F32)
        for part in parts[1:]:
            total = total + part.astype(F32)
        return total.astype(BF16)

    ways = (
        (0, 0, (4, 3, 2, 1), rlp, zp),
        (1, 1, (4, 5, 6, 7), rgm, zm),
        (1, 0, (3, 2, 1), rgp, zp),
        (0, 1, (5, 6, 7), rlm, zm),
    )

    HALF = TOK // 2

    def reduce_step(j):
        for part in range(2):
            rows = slice(part * HALF, (part + 1) * HALF)
            span = pl.ds(part * HALF, HALF)
            for t, way, targets, slots, peer in ways:
                if j >= len(targets):
                    continue
                i = place(targets[j])
                mine, other = ((xg, sibo), (cg, sibg))[t]
                if part == 0:
                    arrived(other.at[i], rsib_r.at[t, i])
                parts = [mine[i, rows, :], other[i, rows, :]]
                if j > 0:
                    arrived(slots.at[j - 1, span], rz_r.at[t, way, j - 1, part])
                    parts.append(slots[j - 1, rows, :])
                mine[i, rows, :] = total_of(parts)
                send(mine.at[i, span], slots.at[j, span], rz_s.at[t, way, j, part], rz_r.at[t, way, j, part], peer)

    def reduce_end():
        i = place(0)
        for part in range(2):
            rows = slice(part * HALF, (part + 1) * HALF)
            span = pl.ds(part * HALF, HALF)
            for t, mine, other, plus, minus, out in ((0, xg, sibo, rlp, rlm, lo_ref), (1, cg, sibg, rgp, rgm, go_ref)):
                np_, nm = (3, 2) if t == 0 else (2, 3)
                if part == 0:
                    arrived(other.at[i], rsib_r.at[t, i])
                arrived(plus.at[np_, span], rz_r.at[t, 0, np_, part])
                arrived(minus.at[nm, span], rz_r.at[t, 1, nm, part])
                out[rows, :] = total_of([mine[i, rows, :], other[i, rows, :], plus[np_, rows, :], minus[nm, rows, :]])

    def gradients(h, way, o):
        gradient(2 * h + way, (yy + o) % NX)

    for way in range(2):
        gradients(0, way, 2)
        far1(0, way, 2)
    for way in range(2):
        gradients(1, way, 2)
        for o in (2, 1, 3, 0):
            far1(1, way, o)
    combine(7, 8)
    combine(5, 7)
    for way in range(2):
        gradients(0, way, 1)
        far1(0, way, 1)
    reduce_step(0)
    for o in (3, 0):
        for way in range(2):
            gradients(0, way, o)
            far1(0, way, o)
    near1(0, 0)
    near1(0, 1)
    gradients(1, 1, 1)
    near1(1, 0)
    gradients(1, 0, 3)
    near1(1, 1)
    gradients(1, 0, 1)
    gradients(1, 1, 3)
    gradients(1, 0, 0)
    gradients(1, 1, 0)
    reduce_step(1)
    for o in (2, 1, 3, 0):
        for h in range(2):
            for way in range(2):
                relay1(h, way, o)
    reduce_step(2)
    for h in range(2):
        settle1(h, 2)
        far2(h)
    reduce_step(3)
    for o, way in ((1, 0), (3, 1)):
        for h in range(2):
            settle1(h, o)
            near2(h, way)
    for h in range(2):
        for way in range(2):
            relay2(h, way)
    settle1(0, 0)
    settle1(1, 0)
    reduce_end()
    settle2(0)
    settle2(1)
    ogu_ref[...] = jnp.swapaxes(fs[:, :, 0:F], 0, 1)
    odn_ref[...] = jnp.swapaxes(fs[:, :, F:W3], 0, 1)
    for copy in sends:
        copy.wait_send()


def move(*refs):
    for n in range(4):
        refs[4 + n][...] = refs[n][...]


def per_device(tokens, routes, gate_weights, cotangent, w_gate_up, w_down):
    vmem = pl.BlockSpec(memory_space=pltpu.VMEM)
    hbm = pl.BlockSpec(memory_space=pl.ANY)
    dma = pltpu.SemaphoreType.DMA
    rows = D // (NX * NX)
    results = pl.pallas_call(
        kernel,
        out_shape=(
            jax.ShapeDtypeStruct((TOK, D), BF16),
            jax.ShapeDtypeStruct((TOK, D), BF16),
            jax.ShapeDtypeStruct((rows, L, F), BF16),
            jax.ShapeDtypeStruct((rows, L, H), BF16),
        ),
        in_specs=[hbm, vmem, vmem, hbm, hbm, hbm],
        out_specs=(vmem, vmem, vmem, vmem),
        scratch_shapes=[
            pltpu.VMEM((L, NX, NX, rows, W3), BF16),
            pltpu.VMEM((256, L, F), BF16),
            pltpu.VMEM((256, L, H), BF16),
            pltpu.VMEM((NZ, 2 * TOK, D), BF16),
            pltpu.VMEM((NZ, 2 * TOK, D), BF16),
            pltpu.VMEM((NZ, 2, 16, TOK), F32),
            pltpu.VMEM((L, SLOTS, D), BF16),
            pltpu.VMEM((L, SLOTS, D), BF16),
            pltpu.VMEM((L, SLOTS, H), BF16),
            pltpu.VMEM((L, SLOTS, F), BF16),
            pltpu.VMEM((L, SLOTS, TOK), F32),
            pltpu.VMEM((NZ, ROWS, 2 * TOK), BF16),
            pltpu.VMEM((NZ, ROWS, D), BF16),
            pltpu.VMEM((NZ, ROWS, D), BF16),
            pltpu.VMEM((NZ, TOK, D), BF16),
            pltpu.VMEM((NZ, TOK, D), BF16),
            pltpu.VMEM((4, TOK, D), BF16),
            pltpu.VMEM((3, TOK, D), BF16),
            pltpu.VMEM((3, TOK, D), BF16),
            pltpu.VMEM((4, TOK, D), BF16),
            pltpu.VMEM((2, 2, NX, rows, W3), BF16),
            pltpu.VMEM((2, 2, 2, NX, rows, W3), BF16),
            pltpu.VMEM((2, 2, rows, W3), BF16),
            pltpu.VMEM((2, 2, 2, rows, W3), BF16),
            pltpu.VMEM((L, rows, W3), BF16),
            dma((3, 2, 4)), dma((3, NZ)), dma((3, NZ)), dma((3, NZ)),
            dma((2, NZ)), dma((2, NZ)), dma((2, 2, 4, 2)), dma((2, 2, 4, 2)),
            dma((2, 2, 9)), dma((2, 2, 9)), dma((2, 2, 3)), dma((2, 2, 3)),
            dma((2,)), dma((2,)),
        ],
        compiler_params=pltpu.CompilerParams(
            collective_id=0, has_side_effects=True, vmem_limit_bytes=63 << 20
        ),
    )(tokens, routes.T, gate_weights.T, cotangent, w_gate_up, w_down)
    return pl.pallas_call(
        move,
        out_shape=tuple(jax.ShapeDtypeStruct(a.shape, a.dtype) for a in results),
        in_specs=[vmem] * 4,
        out_specs=(vmem,) * 4,
    )(*results)


def solution(mesh):
    rows = P(("dp", "expert"), None)
    return jax.shard_map(
        per_device,
        mesh=mesh,
        in_specs=(rows, rows, rows, rows, P(None, "expert", None), P(None, "expert", None)),
        out_specs=(rows, rows, P("dp", "expert", None), P("dp", "expert", None)),
        check_vma=False,
    )
```

```python
import jax
import jax.numpy as jnp
from jax import lax
from jax.experimental import pallas as pl
from jax.experimental.pallas import tpu as pltpu
from jax.sharding import PartitionSpec as P

MESH = pl.DeviceIdType.MESH
F32 = jnp.float32
BF16 = jnp.bfloat16

NZ = 8
NX = 4
TOK = 128
D = 1024
H = 384
F = 2 * H
W3 = 3 * H
L = 4
MOST = 24
PAIR = 2 * MOST
ROWS = L * PAIR
SLOTS = NZ * PAIR


ORDER = (0, 1, 7, 2, 6, 3, 5, 4)


def place(distance):
    return ORDER.index(distance)


def dot(a, b, dims):
    return lax.dot_general(a, b, ((dims[:1], dims[1:]), ((), ())), preferred_element_type=F32)


def kernel(
    x_hbm, rt_ref, gt_ref, c_hbm, wgu_hbm, wdn_hbm,
    lo_ref, go_ref, ogu_ref, odn_ref,
    W, Q, rawg, rawd, xg, cg, mg, Xs, Cs, GH, DP, Gs, Pm, OR, GR,
    sibo, sibg, rlp, rgp, rlm, rgm,
    fwd1, fin1, fwd2, fin2, fs,
    ring_s, ring_r, sib_s, sib_r, rsib_s, rsib_r, rz_s, rz_r, x1_s, x1_r, x2_s, x2_r, raw_sem, own_sem,
):
    dp, ex = lax.axis_index("dp"), lax.axis_index("expert")
    yy, xx = dp // NX, dp % NX
    zz, core = ex // 2, ex % 2

    def at_z(step):
        return (dp, ((zz + step) % NZ) * 2 + core)

    def at_x(step):
        return (yy * NX + (xx + step) % NX, ex)

    def at_y(step):
        return (((yy + step) % NX) * NX + xx, ex)

    zp, zm, sib = at_z(1), at_z(NZ - 1), (dp, zz * 2 + 1 - core)
    xp, xm, yp, ym = at_x(1), at_x(NX - 1), at_y(1), at_y(NX - 1)

    def raw_copies(group):
        rows = pl.ds(group * 256, 256)
        return (
            pltpu.make_async_copy(wgu_hbm.at[rows], rawg, raw_sem.at[0]),
            pltpu.make_async_copy(wdn_hbm.at[rows], rawd, raw_sem.at[1]),
        )

    own_copies = [
        pltpu.make_async_copy(source, gathered.at[place(0), pl.ds(0, TOK)], own_sem.at[n])
        for n, (source, gathered) in enumerate(((x_hbm, xg), (c_hbm, cg)))
    ]
    for copy in own_copies + list(raw_copies(0)):
        copy.start()

    mg[place(0), 0, 0:8, :] = rt_ref[...].astype(F32)
    mg[place(0), 0, 8:16, :] = gt_ref[...]

    barrier = pltpu.get_barrier_semaphore()
    for peer in (zp, zm, sib, xp, xm, yp, ym):
        pl.semaphore_signal(barrier, inc=1, device_id=peer, device_id_type=MESH)
    pl.semaphore_wait(barrier, 7)

    sends, reading = [], {}

    def send(src, dst, send_sem, recv_sem, peer, source_place=None):
        copy = pltpu.make_async_remote_copy(
            src_ref=src, dst_ref=dst, send_sem=send_sem, recv_sem=recv_sem,
            device_id=peer, device_id_type=MESH,
        )
        copy.start()
        (sends if source_place is None else reading.setdefault(source_place, [])).append(copy)

    def arrived(dst, recv_sem):
        pltpu.make_async_remote_copy(
            src_ref=dst, dst_ref=dst, send_sem=recv_sem, recv_sem=recv_sem,
            device_id=zp, device_id_type=MESH,
        ).wait_recv()

    def block(t, distance, column):
        if t == 2:
            return mg.at[place(distance), column]
        return (xg, cg)[t].at[place(distance), pl.ds(column * TOK, TOK)]

    far = {0: (4, 3), 1: (3, 4), 2: (4, 3)}
    mine_of = {0: x_hbm, 1: c_hbm, 2: mg.at[place(0), 0]}
    for t in (2, 0, 1):
        send(mine_of[t], block(t, NZ - 1, 0), ring_s.at[t, 0, 0], ring_r.at[t, NZ - 1], zp)
        send(mine_of[t], block(t, 1, 0), ring_s.at[t, 1, 0], ring_r.at[t, 1], zm)
        send(mine_of[t], block(t, 0, 1), sib_s.at[t, 0], sib_r.at[t, 0], sib)

    def hop(k, tensors):
        for t in tensors:
            for way, distance, peer, further in ((0, NZ - k, zp, NZ - k - 1), (1, k, zm, k + 1)):
                if k > far[t][way]:
                    continue
                arrived(block(t, distance, 0), ring_r.at[t, distance])
                if k < far[t][way]:
                    send(block(t, distance, 0), block(t, further, 0), ring_s.at[t, way, k], ring_r.at[t, further], peer, place(distance))
                send(block(t, distance, 0), block(t, distance, 1), sib_s.at[t, distance], sib_r.at[t, distance], sib, place(distance))

    def relayout(group):
        for copy in raw_copies(group):
            copy.wait()

        def body(i, carry):
            rows = pl.ds(i * 64, 64)
            W[:, group, i, :, 0:F] = jnp.swapaxes(rawg[rows], 0, 1)
            W[:, group, i, :, F:W3] = jnp.swapaxes(rawd[rows], 0, 1)
            return carry

        lax.fori_loop(0, NX, body, 0)
        if group < NX - 1:
            for copy in raw_copies(group + 1):
                copy.start()

    def dispatch(distance):
        for t in (2, 0, 1):
            arrived(block(t, distance, 1), sib_r.at[t, distance])
        i = place(distance)
        first = (ex * L).astype(F32)
        earlier = (
            lax.broadcasted_iota(jnp.int32, (TOK, TOK), 0) < lax.broadcasted_iota(jnp.int32, (TOK, TOK), 1)
        ).astype(BF16)
        slot = lax.broadcasted_iota(jnp.int32, (MOST, TOK), 0).astype(F32)
        sub = lax.broadcasted_iota(jnp.int32, (8, TOK), 0)
        empty = jnp.zeros((MOST, TOK), F32)
        pieces = [[None, None] for _ in range(L)]
        for c in range(2):
            named, gates = mg[i, c, 0:8, :], mg[i, c, 8:16, :]
            masks, weights = [], []
            stacked = jnp.zeros((8, TOK), F32)
            for l in range(L):
                hit = named == first + l
                mask = jnp.sum(hit.astype(F32), axis=0, keepdims=True)
                masks.append(mask)
                weights.append(jnp.sum(jnp.where(hit, gates, 0.0), axis=0, keepdims=True))
                stacked = jnp.where(sub == l, mask, stacked)
            rank = dot(stacked.astype(BF16), earlier, (1, 0))
            for l in range(L):
                chosen = jnp.where((slot == rank[l : l + 1]) & (masks[l] > 0.0), 1.0, 0.0)
                gate = jnp.sum(chosen * weights[l], axis=1, keepdims=True)
                Gs[l, i * PAIR + c * MOST : i * PAIR + (c + 1) * MOST, :] = jnp.broadcast_to(gate, (MOST, TOK))
                pieces[l][c] = jnp.concatenate([chosen, empty] if c == 0 else [empty, chosen], axis=1)
        picked = jnp.concatenate([pieces[l][c] for l in range(L) for c in range(2)], axis=0).astype(BF16)
        Pm[i] = picked
        for gathered, slots in ((xg, Xs), (cg, Cs)):
            got = dot(picked, gathered[i], (1, 0)).astype(BF16)
            for l in range(L):
                slots[l, i * PAIR : (i + 1) * PAIR, :] = got[l * PAIR : (l + 1) * PAIR]

    def inner(i0, i1):
        r0, r1 = i0 * PAIR, i1 * PAIR

        def body(l, carry):
            up_w = W[l, :, :, :, 0:F].reshape(D, F)
            down_w = W[l, :, :, :, F:W3].reshape(D, H)
            gate = Gs[l, r0:r1, 0:1]
            projected = dot(Xs[l, r0:r1], up_w, (1, 0))
            g, u = projected[:, :H], projected[:, H:]
            s = jax.nn.sigmoid(g)
            gs = g * s
            hidden = (gs * u * gate).astype(BF16)
            GH[l, r0:r1] = hidden
            d_hidden = dot(Cs[l, r0:r1], down_w, (1, 0)) * gate
            d_gate = d_hidden * u * s * (1.0 + g * (1.0 - s))
            d_proj = jnp.concatenate([d_gate, d_hidden * gs], axis=1).astype(BF16)
            DP[l, r0:r1] = d_proj
            return carry

        lax.fori_loop(0, L, body, 0)

    def outer(i0, i1):
        r0, r1 = i0 * PAIR, i1 * PAIR

        def body(l, carry):
            out = dot(GH[l, r0:r1], W[l, :, :, :, F:W3].reshape(D, H), (1, 1)).astype(BF16)
            back = dot(DP[l, r0:r1], W[l, :, :, :, 0:F].reshape(D, F), (1, 1)).astype(BF16)
            at = pl.ds(pl.multiple_of(l * PAIR, 16), PAIR)
            for i in range(i0, i1):
                part = slice((i - i0) * PAIR, (i - i0 + 1) * PAIR)
                OR[i, at, :] = out[part]
                GR[i, at, :] = back[part]
            return carry

        lax.fori_loop(0, L, body, 0)

    def combine(i0, i1):
        def body(i, carry):
            picked = Pm[i]
            xg[i] = dot(picked, OR[i], (0, 0)).astype(BF16)
            cg[i] = dot(picked, GR[i], (0, 0)).astype(BF16)
            return carry

        for i in range(i0, i1):
            for copy in reading.pop(i, []):
                copy.wait_send()
        lax.fori_loop(i0, i1, body, 0)
        for i in range(i0, i1):
            send(xg.at[i, pl.ds(TOK, TOK)], sibo.at[i], rsib_s.at[0, i], rsib_r.at[0, i], sib)
            send(cg.at[i, pl.ds(TOK, TOK)], sibg.at[i], rsib_s.at[1, i], rsib_r.at[1, i], sib)

    for group in range(NX):
        relayout(group)
    for copy in own_copies:
        copy.wait()
    hop(1, (2, 0))
    hop(1, (1,))
    for distance in (0, 1, 7):
        dispatch(distance)
    hop(2, (2, 0))
    hop(2, (1,))
    dispatch(2)
    dispatch(6)
    inner(0, 5)
    outer(0, 5)
    hop(3, (2, 0))
    hop(3, (1,))
    combine(0, 5)
    dispatch(3)
    dispatch(5)
    hop(4, (2, 0, 1))
    dispatch(4)
    inner(5, 8)

    def own(l):
        return Q.at[l // 2] if l % 2 == 0 else W.at[l]

    def gradient(l):
        own(l)[:, :, :, 0:F] = dot(Xs[l], DP[l], (0, 0)).astype(BF16).reshape(NX, NX, 64, F)
        own(l)[:, :, :, F:W3] = dot(Cs[l], GH[l], (0, 0)).astype(BF16).reshape(NX, NX, 64, H)

    def gradient_piece(l, q):
        columns = pl.ds(pl.multiple_of(q * 256, 256), 256)
        own(l)[q, :, :, 0:F] = dot(Xs[l, :, columns], DP[l], (0, 0)).astype(BF16).reshape(NX, 64, F)
        own(l)[q, :, :, F:W3] = dot(Cs[l, :, columns], GH[l], (0, 0)).astype(BF16).reshape(NX, 64, H)

    def chunk(h, q, n):
        return (n, q) if h == 0 else (q, n)

    def axes(h, stage):
        along_x = (h == 0) == (stage == 1)
        return (xx, xp, xm) if along_x else (yy, yp, ym)

    def second(h, o):
        return (axes(h, 2)[0] + o) % NX

    def far1(h, way, o):
        at, plus, minus = axes(h, 1)
        n = second(h, o)
        send(
            own(2 * h + way).at[chunk(h, (at + 2) % NX, n)], fwd1.at[h, way, n],
            x1_s.at[h, way, o], x1_r.at[h, way, o], (plus, minus)[way],
        )

    def near1(h, way):
        at, plus, minus = axes(h, 1)
        l, q = 2 * h + 1 - way, (at + (1, 3)[way]) % NX
        source = own(l).at[:, q] if h == 0 else own(l).at[q]
        send(source, fin1.at[h, way, 1 - way], x1_s.at[h, way, 4], x1_r.at[h, way, 4], (plus, minus)[way])

    def relay1(h, way, o):
        at, plus, minus = axes(h, 1)
        n = second(h, o)
        arrived(fwd1.at[h, way, n], x1_r.at[h, way, o])
        mine = own(2 * h + way)[chunk(h, (at + (1, 3)[way]) % NX, n)]
        fwd1[h, way, n] = (fwd1[h, way, n].astype(F32) + mine.astype(F32)).astype(BF16)
        send(
            fwd1.at[h, way, n], fin1.at[h, way, way, n],
            x1_s.at[h, way, 5 + o], x1_r.at[h, way, 5 + o], (plus, minus)[way],
        )

    def settle1(h, o):
        at = axes(h, 1)[0]
        n = second(h, o)
        for way in range(2):
            if o == 2:
                arrived(fin1.at[h, way, 1 - way], x1_r.at[h, way, 4])
            arrived(fin1.at[h, way, way, n], x1_r.at[h, way, 5 + o])
        for slot in range(2):
            held_ref, index = own(2 * h + slot), chunk(h, at, n)
            total = held_ref[index].astype(F32) + fin1[h, 0, slot, n].astype(F32) + fin1[h, 1, slot, n].astype(F32)
            held_ref[index] = total.astype(BF16)

    def held(h, l, q):
        return own(l).at[chunk(h, axes(h, 1)[0], q)]

    def far2(h):
        for way in range(2):
            send(
                held(h, 2 * h + way, second(h, 2)), fwd2.at[h, way],
                x2_s.at[h, way, 0], x2_r.at[h, way, 0], axes(h, 2)[1 + way],
            )

    def near2(h, way):
        send(
            held(h, 2 * h + 1 - way, second(h, (1, 3)[way])), fin2.at[h, way, 1 - way],
            x2_s.at[h, way, 1], x2_r.at[h, way, 1], axes(h, 2)[1 + way],
        )

    def relay2(h, way):
        arrived(fwd2.at[h, way], x2_r.at[h, way, 0])
        mine = held(h, 2 * h + way, second(h, (1, 3)[way]))[...]
        fwd2[h, way] = (fwd2[h, way].astype(F32) + mine.astype(F32)).astype(BF16)
        send(fwd2.at[h, way], fin2.at[h, way, way], x2_s.at[h, way, 2], x2_r.at[h, way, 2], axes(h, 2)[1 + way])

    def settle2(h):
        for way in range(2):
            arrived(fin2.at[h, way, 1 - way], x2_r.at[h, way, 1])
            arrived(fin2.at[h, way, way], x2_r.at[h, way, 2])
        for slot in range(2):
            l = 2 * h + slot
            total = own(l)[yy, xx].astype(F32) + fin2[h, 0, slot].astype(F32) + fin2[h, 1, slot].astype(F32)
            fs[l] = total.astype(BF16)

    def total_of(parts):
        total = parts[0].astype(F32)
        for part in parts[1:]:
            total = total + part.astype(F32)
        return total.astype(BF16)

    ways = (
        (0, 0, (4, 3, 2, 1), rlp, zp),
        (1, 1, (4, 5, 6, 7), rgm, zm),
        (1, 0, (3, 2, 1), rgp, zp),
        (0, 1, (5, 6, 7), rlm, zm),
    )

    HALF = TOK // 2

    def reduce_step(j, part):
        rows = slice(part * HALF, (part + 1) * HALF)
        span = pl.ds(part * HALF, HALF)
        for t, way, targets, slots, peer in ways:
            if j >= len(targets):
                continue
            i = place(targets[j])
            mine, other = ((xg, sibo), (cg, sibg))[t]
            if part == 0:
                arrived(other.at[i], rsib_r.at[t, i])
            parts = [mine[i, rows, :], other[i, rows, :]]
            if j > 0:
                arrived(slots.at[j - 1, span], rz_r.at[t, way, j - 1, part])
                parts.append(slots[j - 1, rows, :])
            mine[i, rows, :] = total_of(parts)
            send(mine.at[i, span], slots.at[j, span], rz_s.at[t, way, j, part], rz_r.at[t, way, j, part], peer)

    def reduce_end(part):
        i = place(0)
        rows = slice(part * HALF, (part + 1) * HALF)
        span = pl.ds(part * HALF, HALF)
        for t, mine, other, plus, minus, out in ((0, xg, sibo, rlp, rlm, lo_ref), (1, cg, sibg, rgp, rgm, go_ref)):
            np_, nm = (3, 2) if t == 0 else (2, 3)
            if part == 0:
                arrived(other.at[i], rsib_r.at[t, i])
            arrived(plus.at[np_, span], rz_r.at[t, 0, np_, part])
            arrived(minus.at[nm, span], rz_r.at[t, 1, nm, part])
            out[rows, :] = total_of([mine[i, rows, :], other[i, rows, :], plus[np_, rows, :], minus[nm, rows, :]])

    gradient(0)
    for o in (2, 1, 3, 0):
        far1(0, 0, o)
    near1(0, 1)
    gradient_piece(2, (yy + 2) % NX)
    for o in (2, 1, 3, 0):
        far1(1, 0, o)
    gradient_piece(2, (yy + 3) % NX)
    near1(1, 1)
    outer(5, 8)
    combine(7, 8)
    combine(5, 7)
    gradient(1)
    for o in (2, 1, 3, 0):
        far1(0, 1, o)
    near1(0, 0)
    reduce_step(0, 0)
    reduce_step(0, 1)
    gradient_piece(2, (yy + 1) % NX)
    gradient_piece(2, yy)
    gradient(3)
    for o in (2, 1, 3, 0):
        far1(1, 1, o)
    near1(1, 0)
    for h in range(2):
        for o in (2, 1, 3, 0):
            relay1(h, 0, o)
    reduce_step(1, 0)
    for h in range(2):
        relay1(h, 1, 2)
    reduce_step(1, 1)
    for o in (1, 3):
        for h in range(2):
            relay1(h, 1, o)
    reduce_step(2, 0)
    for h in range(2):
        relay1(h, 1, 0)
    for h in range(2):
        settle1(h, 2)
        far2(h)
    reduce_step(2, 1)
    for o, way in ((1, 0), (3, 1)):
        for h in range(2):
            settle1(h, o)
            near2(h, way)
    reduce_step(3, 0)
    for h in range(2):
        settle1(h, 0)
    for h in range(2):
        for way in range(2):
            relay2(h, way)
    reduce_step(3, 1)
    reduce_end(0)
    settle2(0)
    settle2(1)
    reduce_end(1)
    ogu_ref[...] = jnp.swapaxes(fs[:, :, 0:F], 0, 1)
    odn_ref[...] = jnp.swapaxes(fs[:, :, F:W3], 0, 1)
    for copy in sends:
        copy.wait_send()


def move(*refs):
    for n in range(4):
        refs[4 + n][...] = refs[n][...]


def per_device(tokens, routes, gate_weights, cotangent, w_gate_up, w_down):
    vmem = pl.BlockSpec(memory_space=pltpu.VMEM)
    hbm = pl.BlockSpec(memory_space=pl.ANY)
    dma = pltpu.SemaphoreType.DMA
    rows = D // (NX * NX)
    results = pl.pallas_call(
        kernel,
        out_shape=(
            jax.ShapeDtypeStruct((TOK, D), BF16),
            jax.ShapeDtypeStruct((TOK, D), BF16),
            jax.ShapeDtypeStruct((rows, L, F), BF16),
            jax.ShapeDtypeStruct((rows, L, H), BF16),
        ),
        in_specs=[hbm, vmem, vmem, hbm, hbm, hbm],
        out_specs=(vmem, vmem, vmem, vmem),
        scratch_shapes=[
            pltpu.VMEM((L, NX, NX, rows, W3), BF16),
            pltpu.VMEM((2, NX, NX, rows, W3), BF16),
            pltpu.VMEM((256, L, F), BF16),
            pltpu.VMEM((256, L, H), BF16),
            pltpu.VMEM((NZ, 2 * TOK, D), BF16),
            pltpu.VMEM((NZ, 2 * TOK, D), BF16),
            pltpu.VMEM((NZ, 2, 16, TOK), F32),
            pltpu.VMEM((L, SLOTS, D), BF16),
            pltpu.VMEM((L, SLOTS, D), BF16),
            pltpu.VMEM((L, SLOTS, H), BF16),
            pltpu.VMEM((L, SLOTS, F), BF16),
            pltpu.VMEM((L, SLOTS, TOK), F32),
            pltpu.VMEM((NZ, ROWS, 2 * TOK), BF16),
            pltpu.VMEM((NZ, ROWS, D), BF16),
            pltpu.VMEM((NZ, ROWS, D), BF16),
            pltpu.VMEM((NZ, TOK, D), BF16),
            pltpu.VMEM((NZ, TOK, D), BF16),
            pltpu.VMEM((4, TOK, D), BF16),
            pltpu.VMEM((3, TOK, D), BF16),
            pltpu.VMEM((3, TOK, D), BF16),
            pltpu.VMEM((4, TOK, D), BF16),
            pltpu.VMEM((2, 2, NX, rows, W3), BF16),
            pltpu.VMEM((2, 2, 2, NX, rows, W3), BF16),
            pltpu.VMEM((2, 2, rows, W3), BF16),
            pltpu.VMEM((2, 2, 2, rows, W3), BF16),
            pltpu.VMEM((L, rows, W3), BF16),
            dma((3, 2, 4)), dma((3, NZ)), dma((3, NZ)), dma((3, NZ)),
            dma((2, NZ)), dma((2, NZ)), dma((2, 2, 4, 2)), dma((2, 2, 4, 2)),
            dma((2, 2, 9)), dma((2, 2, 9)), dma((2, 2, 3)), dma((2, 2, 3)),
            dma((2,)), dma((2,)),
        ],
        compiler_params=pltpu.CompilerParams(
            collective_id=0, has_side_effects=True, vmem_limit_bytes=63 << 20
        ),
    )(tokens, routes.T, gate_weights.T, cotangent, w_gate_up, w_down)
    return pl.pallas_call(
        move,
        out_shape=tuple(jax.ShapeDtypeStruct(a.shape, a.dtype) for a in results),
        in_specs=[vmem] * 4,
        out_specs=(vmem,) * 4,
    )(*results)


def solution(mesh):
    rows = P(("dp", "expert"), None)
    return jax.shard_map(
        per_device,
        mesh=mesh,
        in_specs=(rows, rows, rows, rows, P(None, "expert", None), P(None, "expert", None)),
        out_specs=(rows, rows, P("dp", "expert", None), P("dp", "expert", None)),
        check_vma=False,
    )
```

```python
import jax
import jax.numpy as jnp
from jax import lax
from jax.experimental import pallas as pl
from jax.experimental.pallas import tpu as pltpu
from jax.sharding import PartitionSpec as P

MESH = pl.DeviceIdType.MESH
F32 = jnp.float32
BF16 = jnp.bfloat16

NZ = 8
NX = 4
TOK = 128
D = 1024
H = 384
F = 2 * H
W3 = 3 * H
L = 4
MOST = 24
PAIR = 2 * MOST
ROWS = L * PAIR
SLOTS = NZ * PAIR


ORDER = (0, 1, 7, 2, 6, 3, 5, 4)


def place(distance):
    return ORDER.index(distance)


def dot(a, b, dims):
    return lax.dot_general(a, b, ((dims[:1], dims[1:]), ((), ())), preferred_element_type=F32)


def kernel(
    x_hbm, rt_ref, gt_ref, c_hbm, wgu_hbm, wdn_hbm,
    lo_ref, go_ref, ogu_ref, odn_ref,
    W, Q, rawg, rawd, xg, cg, mg, Xs, Cs, GH, DP, Gs, Pm, OR, GR,
    sibo, sibg, rlp, rgp, rlm, rgm,
    fwd1, fin1, fwd2, fin2, fs,
    ring_s, ring_r, sib_s, sib_r, rsib_s, rsib_r, rz_s, rz_r, x1_s, x1_r, x2_s, x2_r, raw_sem, own_sem,
):
    dp, ex = lax.axis_index("dp"), lax.axis_index("expert")
    yy, xx = dp // NX, dp % NX
    zz, core = ex // 2, ex % 2

    def at_z(step):
        return (dp, ((zz + step) % NZ) * 2 + core)

    def at_x(step):
        return (yy * NX + (xx + step) % NX, ex)

    def at_y(step):
        return (((yy + step) % NX) * NX + xx, ex)

    zp, zm, sib = at_z(1), at_z(NZ - 1), (dp, zz * 2 + 1 - core)
    xp, xm, yp, ym = at_x(1), at_x(NX - 1), at_y(1), at_y(NX - 1)

    def raw_copies(group):
        rows = pl.ds(group * 256, 256)
        return (
            pltpu.make_async_copy(wgu_hbm.at[rows], rawg, raw_sem.at[0]),
            pltpu.make_async_copy(wdn_hbm.at[rows], rawd, raw_sem.at[1]),
        )

    own_copies = [
        pltpu.make_async_copy(source, gathered.at[place(0), pl.ds(0, TOK)], own_sem.at[n])
        for n, (source, gathered) in enumerate(((x_hbm, xg), (c_hbm, cg)))
    ]
    for copy in own_copies + list(raw_copies(0)):
        copy.start()

    mg[place(0), 0, 0:8, :] = rt_ref[...].astype(F32)
    mg[place(0), 0, 8:16, :] = gt_ref[...]

    barrier = pltpu.get_barrier_semaphore()
    for peer in (zp, zm, sib, xp, xm, yp, ym):
        pl.semaphore_signal(barrier, inc=1, device_id=peer, device_id_type=MESH)
    pl.semaphore_wait(barrier, 7)

    sends, reading = [], {}

    def send(src, dst, send_sem, recv_sem, peer, source_place=None):
        copy = pltpu.make_async_remote_copy(
            src_ref=src, dst_ref=dst, send_sem=send_sem, recv_sem=recv_sem,
            device_id=peer, device_id_type=MESH,
        )
        copy.start()
        (sends if source_place is None else reading.setdefault(source_place, [])).append(copy)

    def arrived(dst, recv_sem):
        pltpu.make_async_remote_copy(
            src_ref=dst, dst_ref=dst, send_sem=recv_sem, recv_sem=recv_sem,
            device_id=zp, device_id_type=MESH,
        ).wait_recv()

    def block(t, distance, column):
        if t == 2:
            return mg.at[place(distance), column]
        return (xg, cg)[t].at[place(distance), pl.ds(column * TOK, TOK)]

    far = {0: (4, 3), 1: (3, 4), 2: (4, 3)}
    mine_of = {0: x_hbm, 1: c_hbm, 2: mg.at[place(0), 0]}
    for t in (2, 0, 1):
        send(mine_of[t], block(t, NZ - 1, 0), ring_s.at[t, 0, 0], ring_r.at[t, NZ - 1], zp)
        send(mine_of[t], block(t, 1, 0), ring_s.at[t, 1, 0], ring_r.at[t, 1], zm)
        send(mine_of[t], block(t, 0, 1), sib_s.at[t, 0], sib_r.at[t, 0], sib)

    def hop(k, tensors):
        for t in tensors:
            for way, distance, peer, further in ((0, NZ - k, zp, NZ - k - 1), (1, k, zm, k + 1)):
                if k > far[t][way]:
                    continue
                arrived(block(t, distance, 0), ring_r.at[t, distance])
                if k < far[t][way]:
                    send(block(t, distance, 0), block(t, further, 0), ring_s.at[t, way, k], ring_r.at[t, further], peer, place(distance))
                send(block(t, distance, 0), block(t, distance, 1), sib_s.at[t, distance], sib_r.at[t, distance], sib, place(distance))

    def relayout(group):
        for copy in raw_copies(group):
            copy.wait()

        def body(i, carry):
            rows = pl.ds(i * 64, 64)
            W[:, group, i, :, 0:F] = jnp.swapaxes(rawg[rows], 0, 1)
            W[:, group, i, :, F:W3] = jnp.swapaxes(rawd[rows], 0, 1)
            return carry

        lax.fori_loop(0, NX, body, 0)
        if group < NX - 1:
            for copy in raw_copies(group + 1):
                copy.start()

    def dispatch(distance):
        for t in (2, 0, 1):
            arrived(block(t, distance, 1), sib_r.at[t, distance])
        i = place(distance)
        first = (ex * L).astype(F32)
        earlier = (
            lax.broadcasted_iota(jnp.int32, (TOK, TOK), 0) < lax.broadcasted_iota(jnp.int32, (TOK, TOK), 1)
        ).astype(BF16)
        slot = lax.broadcasted_iota(jnp.int32, (MOST, TOK), 0).astype(F32)
        sub = lax.broadcasted_iota(jnp.int32, (8, TOK), 0)
        empty = jnp.zeros((MOST, TOK), F32)
        pieces = [[None, None] for _ in range(L)]
        for c in range(2):
            named, gates = mg[i, c, 0:8, :], mg[i, c, 8:16, :]
            masks, weights = [], []
            stacked = jnp.zeros((8, TOK), F32)
            for l in range(L):
                hit = named == first + l
                mask = jnp.sum(hit.astype(F32), axis=0, keepdims=True)
                masks.append(mask)
                weights.append(jnp.sum(jnp.where(hit, gates, 0.0), axis=0, keepdims=True))
                stacked = jnp.where(sub == l, mask, stacked)
            rank = dot(stacked.astype(BF16), earlier, (1, 0))
            for l in range(L):
                chosen = jnp.where((slot == rank[l : l + 1]) & (masks[l] > 0.0), 1.0, 0.0)
                gate = jnp.sum(chosen * weights[l], axis=1, keepdims=True)
                Gs[l, i * PAIR + c * MOST : i * PAIR + (c + 1) * MOST, :] = jnp.broadcast_to(gate, (MOST, TOK))
                pieces[l][c] = jnp.concatenate([chosen, empty] if c == 0 else [empty, chosen], axis=1)
        picked = jnp.concatenate([pieces[l][c] for l in range(L) for c in range(2)], axis=0).astype(BF16)
        Pm[i] = picked
        for gathered, slots in ((xg, Xs), (cg, Cs)):
            got = dot(picked, gathered[i], (1, 0)).astype(BF16)
            for l in range(L):
                slots[l, i * PAIR : (i + 1) * PAIR, :] = got[l * PAIR : (l + 1) * PAIR]

    def inner(i0, i1, l0=0, l1=L):
        r0, r1 = i0 * PAIR, i1 * PAIR

        def body(l, carry):
            up_w = W[l, :, :, :, 0:F].reshape(D, F)
            down_w = W[l, :, :, :, F:W3].reshape(D, H)
            gate = Gs[l, r0:r1, 0:1]
            projected = dot(Xs[l, r0:r1], up_w, (1, 0))
            g, u = projected[:, :H], projected[:, H:]
            s = jax.nn.sigmoid(g)
            gs = g * s
            hidden = (gs * u * gate).astype(BF16)
            GH[l, r0:r1] = hidden
            d_hidden = dot(Cs[l, r0:r1], down_w, (1, 0)) * gate
            d_gate = d_hidden * u * s * (1.0 + g * (1.0 - s))
            d_proj = jnp.concatenate([d_gate, d_hidden * gs], axis=1).astype(BF16)
            DP[l, r0:r1] = d_proj
            return carry

        lax.fori_loop(l0, l1, body, 0)

    def outer(i0, i1):
        r0, r1 = i0 * PAIR, i1 * PAIR

        def body(l, carry):
            out = dot(GH[l, r0:r1], W[l, :, :, :, F:W3].reshape(D, H), (1, 1)).astype(BF16)
            back = dot(DP[l, r0:r1], W[l, :, :, :, 0:F].reshape(D, F), (1, 1)).astype(BF16)
            at = pl.ds(pl.multiple_of(l * PAIR, 16), PAIR)
            for i in range(i0, i1):
                part = slice((i - i0) * PAIR, (i - i0 + 1) * PAIR)
                OR[i, at, :] = out[part]
                GR[i, at, :] = back[part]
            return carry

        lax.fori_loop(0, L, body, 0)

    def combine(i0, i1):
        def body(i, carry):
            picked = Pm[i]
            xg[i] = dot(picked, OR[i], (0, 0)).astype(BF16)
            cg[i] = dot(picked, GR[i], (0, 0)).astype(BF16)
            return carry

        for i in range(i0, i1):
            for copy in reading.pop(i, []):
                copy.wait_send()
        lax.fori_loop(i0, i1, body, 0)
        for i in range(i0, i1):
            send(xg.at[i, pl.ds(TOK, TOK)], sibo.at[i], rsib_s.at[0, i], rsib_r.at[0, i], sib)
            send(cg.at[i, pl.ds(TOK, TOK)], sibg.at[i], rsib_s.at[1, i], rsib_r.at[1, i], sib)

    for group in range(NX):
        relayout(group)
    for copy in own_copies:
        copy.wait()
    hop(1, (2, 0))
    hop(1, (1,))
    for distance in (0, 1, 7):
        dispatch(distance)
    hop(2, (2, 0))
    hop(2, (1,))
    dispatch(2)
    dispatch(6)
    inner(0, 5)
    outer(0, 5)
    hop(3, (2, 0))
    hop(3, (1,))
    combine(0, 5)
    dispatch(3)
    dispatch(5)
    hop(4, (2, 0, 1))
    dispatch(4)

    def own(l):
        return Q.at[l // 2] if l % 2 == 0 else W.at[l]

    def gradient(l):
        own(l)[:, :, :, 0:F] = dot(Xs[l], DP[l], (0, 0)).astype(BF16).reshape(NX, NX, 64, F)
        own(l)[:, :, :, F:W3] = dot(Cs[l], GH[l], (0, 0)).astype(BF16).reshape(NX, NX, 64, H)

    def gradient_piece(l, q):
        columns = pl.ds(pl.multiple_of(q * 256, 256), 256)
        own(l)[q, :, :, 0:F] = dot(Xs[l, :, columns], DP[l], (0, 0)).astype(BF16).reshape(NX, 64, F)
        own(l)[q, :, :, F:W3] = dot(Cs[l, :, columns], GH[l], (0, 0)).astype(BF16).reshape(NX, 64, H)

    def chunk(h, q, n):
        return (n, q) if h == 0 else (q, n)

    def axes(h, stage):
        along_x = (h == 0) == (stage == 1)
        return (xx, xp, xm) if along_x else (yy, yp, ym)

    def second(h, o):
        return (axes(h, 2)[0] + o) % NX

    def far1(h, way, o):
        at, plus, minus = axes(h, 1)
        n = second(h, o)
        send(
            own(2 * h + way).at[chunk(h, (at + 2) % NX, n)], fwd1.at[h, way, n],
            x1_s.at[h, way, o], x1_r.at[h, way, o], (plus, minus)[way],
        )

    def near1(h, way):
        at, plus, minus = axes(h, 1)
        l, q = 2 * h + 1 - way, (at + (1, 3)[way]) % NX
        source = own(l).at[:, q] if h == 0 else own(l).at[q]
        send(source, fin1.at[h, way, 1 - way], x1_s.at[h, way, 4], x1_r.at[h, way, 4], (plus, minus)[way])

    def relay1(h, way, o):
        at, plus, minus = axes(h, 1)
        n = second(h, o)
        arrived(fwd1.at[h, way, n], x1_r.at[h, way, o])
        mine = own(2 * h + way)[chunk(h, (at + (1, 3)[way]) % NX, n)]
        fwd1[h, way, n] = (fwd1[h, way, n].astype(F32) + mine.astype(F32)).astype(BF16)
        send(
            fwd1.at[h, way, n], fin1.at[h, way, way, n],
            x1_s.at[h, way, 5 + o], x1_r.at[h, way, 5 + o], (plus, minus)[way],
        )

    def settle1(h, o):
        at = axes(h, 1)[0]
        n = second(h, o)
        for way in range(2):
            if o == 2:
                arrived(fin1.at[h, way, 1 - way], x1_r.at[h, way, 4])
            arrived(fin1.at[h, way, way, n], x1_r.at[h, way, 5 + o])
        for slot in range(2):
            held_ref, index = own(2 * h + slot), chunk(h, at, n)
            total = held_ref[index].astype(F32) + fin1[h, 0, slot, n].astype(F32) + fin1[h, 1, slot, n].astype(F32)
            held_ref[index] = total.astype(BF16)

    def held(h, l, q):
        return own(l).at[chunk(h, axes(h, 1)[0], q)]

    def far2(h):
        for way in range(2):
            send(
                held(h, 2 * h + way, second(h, 2)), fwd2.at[h, way],
                x2_s.at[h, way, 0], x2_r.at[h, way, 0], axes(h, 2)[1 + way],
            )

    def near2(h, way):
        send(
            held(h, 2 * h + 1 - way, second(h, (1, 3)[way])), fin2.at[h, way, 1 - way],
            x2_s.at[h, way, 1], x2_r.at[h, way, 1], axes(h, 2)[1 + way],
        )

    def relay2(h, way):
        arrived(fwd2.at[h, way], x2_r.at[h, way, 0])
        mine = held(h, 2 * h + way, second(h, (1, 3)[way]))[...]
        fwd2[h, way] = (fwd2[h, way].astype(F32) + mine.astype(F32)).astype(BF16)
        send(fwd2.at[h, way], fin2.at[h, way, way], x2_s.at[h, way, 2], x2_r.at[h, way, 2], axes(h, 2)[1 + way])

    def settle2(h):
        for way in range(2):
            arrived(fin2.at[h, way, 1 - way], x2_r.at[h, way, 1])
            arrived(fin2.at[h, way, way], x2_r.at[h, way, 2])
        for slot in range(2):
            l = 2 * h + slot
            total = own(l)[yy, xx].astype(F32) + fin2[h, 0, slot].astype(F32) + fin2[h, 1, slot].astype(F32)
            fs[l] = total.astype(BF16)

    def total_of(parts):
        total = parts[0].astype(F32)
        for part in parts[1:]:
            total = total + part.astype(F32)
        return total.astype(BF16)

    ways = (
        (0, 0, (4, 3, 2, 1), rlp, zp),
        (1, 1, (4, 5, 6, 7), rgm, zm),
        (1, 0, (3, 2, 1), rgp, zp),
        (0, 1, (5, 6, 7), rlm, zm),
    )

    HALF = TOK // 2

    def reduce_step(j, part):
        rows = slice(part * HALF, (part + 1) * HALF)
        span = pl.ds(part * HALF, HALF)
        for t, way, targets, slots, peer in ways:
            if j >= len(targets):
                continue
            i = place(targets[j])
            mine, other = ((xg, sibo), (cg, sibg))[t]
            if part == 0:
                arrived(other.at[i], rsib_r.at[t, i])
            parts = [mine[i, rows, :], other[i, rows, :]]
            if j > 0:
                arrived(slots.at[j - 1, span], rz_r.at[t, way, j - 1, part])
                parts.append(slots[j - 1, rows, :])
            mine[i, rows, :] = total_of(parts)
            send(mine.at[i, span], slots.at[j, span], rz_s.at[t, way, j, part], rz_r.at[t, way, j, part], peer)

    def reduce_end(part):
        i = place(0)
        rows = slice(part * HALF, (part + 1) * HALF)
        span = pl.ds(part * HALF, HALF)
        for t, mine, other, plus, minus, out in ((0, xg, sibo, rlp, rlm, lo_ref), (1, cg, sibg, rgp, rgm, go_ref)):
            np_, nm = (3, 2) if t == 0 else (2, 3)
            if part == 0:
                arrived(other.at[i], rsib_r.at[t, i])
            arrived(plus.at[np_, span], rz_r.at[t, 0, np_, part])
            arrived(minus.at[nm, span], rz_r.at[t, 1, nm, part])
            out[rows, :] = total_of([mine[i, rows, :], other[i, rows, :], plus[np_, rows, :], minus[nm, rows, :]])

    inner(5, 8, 0, 1)
    gradient(0)
    for o in (2, 1, 3, 0):
        far1(0, 0, o)
    near1(0, 1)
    inner(5, 8, 2, 3)
    gradient_piece(2, (yy + 2) % NX)
    for o in (2, 1, 3, 0):
        far1(1, 0, o)
    gradient_piece(2, (yy + 3) % NX)
    near1(1, 1)
    inner(5, 8, 1, 2)
    inner(5, 8, 3, 4)
    outer(5, 8)
    combine(7, 8)
    combine(5, 7)
    reduce_step(0, 0)
    reduce_step(0, 1)
    gradient(1)
    for o in (2, 1, 3, 0):
        far1(0, 1, o)
    near1(0, 0)
    gradient(3)
    for o in (2, 1, 3, 0):
        far1(1, 1, o)
    near1(1, 0)
    gradient_piece(2, (yy + 1) % NX)
    gradient_piece(2, yy)
    for h in range(2):
        for o in (2, 1, 3, 0):
            relay1(h, 0, o)
    reduce_step(1, 0)
    for h in range(2):
        relay1(h, 1, 2)
    reduce_step(1, 1)
    for o in (1, 3):
        for h in range(2):
            relay1(h, 1, o)
    reduce_step(2, 0)
    for h in range(2):
        relay1(h, 1, 0)
    for h in range(2):
        settle1(h, 2)
        far2(h)
    reduce_step(2, 1)
    for o, way in ((1, 0), (3, 1)):
        for h in range(2):
            settle1(h, o)
            near2(h, way)
    reduce_step(3, 0)
    for h in range(2):
        settle1(h, 0)
    for h in range(2):
        for way in range(2):
            relay2(h, way)
    reduce_step(3, 1)
    reduce_end(0)
    settle2(0)
    settle2(1)
    reduce_end(1)
    ogu_ref[...] = jnp.swapaxes(fs[:, :, 0:F], 0, 1)
    odn_ref[...] = jnp.swapaxes(fs[:, :, F:W3], 0, 1)
    for copy in sends:
        copy.wait_send()


def move(*refs):
    for n in range(4):
        refs[4 + n][...] = refs[n][...]


def per_device(tokens, routes, gate_weights, cotangent, w_gate_up, w_down):
    vmem = pl.BlockSpec(memory_space=pltpu.VMEM)
    hbm = pl.BlockSpec(memory_space=pl.ANY)
    dma = pltpu.SemaphoreType.DMA
    rows = D // (NX * NX)
    results = pl.pallas_call(
        kernel,
        out_shape=(
            jax.ShapeDtypeStruct((TOK, D), BF16),
            jax.ShapeDtypeStruct((TOK, D), BF16),
            jax.ShapeDtypeStruct((rows, L, F), BF16),
            jax.ShapeDtypeStruct((rows, L, H), BF16),
        ),
        in_specs=[hbm, vmem, vmem, hbm, hbm, hbm],
        out_specs=(vmem, vmem, vmem, vmem),
        scratch_shapes=[
            pltpu.VMEM((L, NX, NX, rows, W3), BF16),
            pltpu.VMEM((2, NX, NX, rows, W3), BF16),
            pltpu.VMEM((256, L, F), BF16),
            pltpu.VMEM((256, L, H), BF16),
            pltpu.VMEM((NZ, 2 * TOK, D), BF16),
            pltpu.VMEM((NZ, 2 * TOK, D), BF16),
            pltpu.VMEM((NZ, 2, 16, TOK), F32),
            pltpu.VMEM((L, SLOTS, D), BF16),
            pltpu.VMEM((L, SLOTS, D), BF16),
            pltpu.VMEM((L, SLOTS, H), BF16),
            pltpu.VMEM((L, SLOTS, F), BF16),
            pltpu.VMEM((L, SLOTS, TOK), F32),
            pltpu.VMEM((NZ, ROWS, 2 * TOK), BF16),
            pltpu.VMEM((NZ, ROWS, D), BF16),
            pltpu.VMEM((NZ, ROWS, D), BF16),
            pltpu.VMEM((NZ, TOK, D), BF16),
            pltpu.VMEM((NZ, TOK, D), BF16),
            pltpu.VMEM((4, TOK, D), BF16),
            pltpu.VMEM((3, TOK, D), BF16),
            pltpu.VMEM((3, TOK, D), BF16),
            pltpu.VMEM((4, TOK, D), BF16),
            pltpu.VMEM((2, 2, NX, rows, W3), BF16),
            pltpu.VMEM((2, 2, 2, NX, rows, W3), BF16),
            pltpu.VMEM((2, 2, rows, W3), BF16),
            pltpu.VMEM((2, 2, 2, rows, W3), BF16),
            pltpu.VMEM((L, rows, W3), BF16),
            dma((3, 2, 4)), dma((3, NZ)), dma((3, NZ)), dma((3, NZ)),
            dma((2, NZ)), dma((2, NZ)), dma((2, 2, 4, 2)), dma((2, 2, 4, 2)),
            dma((2, 2, 9)), dma((2, 2, 9)), dma((2, 2, 3)), dma((2, 2, 3)),
            dma((2,)), dma((2,)),
        ],
        compiler_params=pltpu.CompilerParams(
            collective_id=0, has_side_effects=True, vmem_limit_bytes=63 << 20
        ),
    )(tokens, routes.T, gate_weights.T, cotangent, w_gate_up, w_down)
    return pl.pallas_call(
        move,
        out_shape=tuple(jax.ShapeDtypeStruct(a.shape, a.dtype) for a in results),
        in_specs=[vmem] * 4,
        out_specs=(vmem,) * 4,
    )(*results)


def solution(mesh):
    rows = P(("dp", "expert"), None)
    return jax.shard_map(
        per_device,
        mesh=mesh,
        in_specs=(rows, rows, rows, rows, P(None, "expert", None), P(None, "expert", None)),
        out_specs=(rows, rows, P("dp", "expert", None), P("dp", "expert", None)),
        check_vma=False,
    )
```

```python
import jax
import jax.numpy as jnp
from jax import lax
from jax.experimental import pallas as pl
from jax.experimental.pallas import tpu as pltpu
from jax.sharding import PartitionSpec as P

MESH = pl.DeviceIdType.MESH
F32 = jnp.float32
BF16 = jnp.bfloat16

NZ = 8
NX = 4
TOK = 128
D = 1024
H = 384
F = 2 * H
W3 = 3 * H
L = 4
MOST = 24
PAIR = 2 * MOST
ROWS = L * PAIR
SLOTS = NZ * PAIR


ORDER = (0, 1, 7, 2, 6, 3, 5, 4)


def place(distance):
    return ORDER.index(distance)


def dot(a, b, dims):
    return lax.dot_general(a, b, ((dims[:1], dims[1:]), ((), ())), preferred_element_type=F32)


def kernel(
    x_hbm, rt_ref, gt_ref, c_hbm, wgu_hbm, wdn_hbm,
    lo_ref, go_ref, ogu_ref, odn_ref,
    W, Q, rawg, rawd, xg, cg, mg, Xs, Cs, GH, DP, Gs, Pm, OR, GR,
    sibo, sibg, rlp, rgp, rlm, rgm,
    fwd1, fin1, fwd2, fin2, fs,
    ring_s, ring_r, sib_s, sib_r, rsib_s, rsib_r, rz_s, rz_r, x1_s, x1_r, x2_s, x2_r, raw_sem, own_sem,
):
    dp, ex = lax.axis_index("dp"), lax.axis_index("expert")
    yy, xx = dp // NX, dp % NX
    zz, core = ex // 2, ex % 2

    def at_z(step):
        return (dp, ((zz + step) % NZ) * 2 + core)

    def at_x(step):
        return (yy * NX + (xx + step) % NX, ex)

    def at_y(step):
        return (((yy + step) % NX) * NX + xx, ex)

    zp, zm, sib = at_z(1), at_z(NZ - 1), (dp, zz * 2 + 1 - core)
    xp, xm, yp, ym = at_x(1), at_x(NX - 1), at_y(1), at_y(NX - 1)

    def raw_copies(group):
        rows = pl.ds(group * 256, 256)
        return (
            pltpu.make_async_copy(wgu_hbm.at[rows], rawg, raw_sem.at[0]),
            pltpu.make_async_copy(wdn_hbm.at[rows], rawd, raw_sem.at[1]),
        )

    own_copies = [
        pltpu.make_async_copy(source, gathered.at[place(0), pl.ds(0, TOK)], own_sem.at[n])
        for n, (source, gathered) in enumerate(((x_hbm, xg), (c_hbm, cg)))
    ]
    for copy in own_copies + list(raw_copies(0)):
        copy.start()

    mg[place(0), 0, 0:8, :] = rt_ref[...].astype(F32)
    mg[place(0), 0, 8:16, :] = gt_ref[...]

    barrier = pltpu.get_barrier_semaphore()
    for peer in (zp, zm, sib, xp, xm, yp, ym):
        pl.semaphore_signal(barrier, inc=1, device_id=peer, device_id_type=MESH)
    pl.semaphore_wait(barrier, 7)

    sends, reading = [], {}

    def send(src, dst, send_sem, recv_sem, peer, source_place=None):
        copy = pltpu.make_async_remote_copy(
            src_ref=src, dst_ref=dst, send_sem=send_sem, recv_sem=recv_sem,
            device_id=peer, device_id_type=MESH,
        )
        copy.start()
        (sends if source_place is None else reading.setdefault(source_place, [])).append(copy)

    def arrived(dst, recv_sem):
        pltpu.make_async_remote_copy(
            src_ref=dst, dst_ref=dst, send_sem=recv_sem, recv_sem=recv_sem,
            device_id=zp, device_id_type=MESH,
        ).wait_recv()

    def block(t, distance, column):
        if t == 2:
            return mg.at[place(distance), column]
        return (xg, cg)[t].at[place(distance), pl.ds(column * TOK, TOK)]

    far = {0: (4, 3), 1: (3, 4), 2: (4, 3)}
    mine_of = {0: x_hbm, 1: c_hbm, 2: mg.at[place(0), 0]}
    for t in (2, 0, 1):
        send(mine_of[t], block(t, NZ - 1, 0), ring_s.at[t, 0, 0], ring_r.at[t, NZ - 1], zp)
        send(mine_of[t], block(t, 1, 0), ring_s.at[t, 1, 0], ring_r.at[t, 1], zm)
        send(mine_of[t], block(t, 0, 1), sib_s.at[t, 0], sib_r.at[t, 0], sib)

    def hop(k, tensors):
        for t in tensors:
            for way, distance, peer, further in ((0, NZ - k, zp, NZ - k - 1), (1, k, zm, k + 1)):
                if k > far[t][way]:
                    continue
                arrived(block(t, distance, 0), ring_r.at[t, distance])
                if k < far[t][way]:
                    send(block(t, distance, 0), block(t, further, 0), ring_s.at[t, way, k], ring_r.at[t, further], peer, place(distance))
                send(block(t, distance, 0), block(t, distance, 1), sib_s.at[t, distance], sib_r.at[t, distance], sib, place(distance))

    def relayout(group):
        for copy in raw_copies(group):
            copy.wait()

        def body(i, carry):
            rows = pl.ds(i * 64, 64)
            W[:, group, i, :, 0:F] = jnp.swapaxes(rawg[rows], 0, 1)
            W[:, group, i, :, F:W3] = jnp.swapaxes(rawd[rows], 0, 1)
            return carry

        lax.fori_loop(0, NX, body, 0)
        if group < NX - 1:
            for copy in raw_copies(group + 1):
                copy.start()

    def dispatch(distance):
        for t in (2, 0, 1):
            arrived(block(t, distance, 1), sib_r.at[t, distance])
        i = place(distance)
        first = (ex * L).astype(F32)
        earlier = (
            lax.broadcasted_iota(jnp.int32, (TOK, TOK), 0) < lax.broadcasted_iota(jnp.int32, (TOK, TOK), 1)
        ).astype(BF16)
        slot = lax.broadcasted_iota(jnp.int32, (MOST, TOK), 0).astype(F32)
        sub = lax.broadcasted_iota(jnp.int32, (8, TOK), 0)
        empty = jnp.zeros((MOST, TOK), F32)
        pieces = [[None, None] for _ in range(L)]
        for c in range(2):
            named, gates = mg[i, c, 0:8, :], mg[i, c, 8:16, :]
            masks, weights = [], []
            stacked = jnp.zeros((8, TOK), F32)
            for l in range(L):
                hit = named == first + l
                mask = jnp.sum(hit.astype(F32), axis=0, keepdims=True)
                masks.append(mask)
                weights.append(jnp.sum(jnp.where(hit, gates, 0.0), axis=0, keepdims=True))
                stacked = jnp.where(sub == l, mask, stacked)
            rank = dot(stacked.astype(BF16), earlier, (1, 0))
            for l in range(L):
                chosen = jnp.where((slot == rank[l : l + 1]) & (masks[l] > 0.0), 1.0, 0.0)
                gate = jnp.sum(chosen * weights[l], axis=1, keepdims=True)
                Gs[l, i * PAIR + c * MOST : i * PAIR + (c + 1) * MOST, :] = jnp.broadcast_to(gate, (MOST, TOK))
                pieces[l][c] = jnp.concatenate([chosen, empty] if c == 0 else [empty, chosen], axis=1)
        picked = jnp.concatenate([pieces[l][c] for l in range(L) for c in range(2)], axis=0).astype(BF16)
        Pm[i] = picked
        for gathered, slots in ((xg, Xs), (cg, Cs)):
            got = dot(picked, gathered[i], (1, 0)).astype(BF16)
            for l in range(L):
                slots[l, i * PAIR : (i + 1) * PAIR, :] = got[l * PAIR : (l + 1) * PAIR]

    def inner(i0, i1, l0=0, l1=L):
        r0, r1 = i0 * PAIR, i1 * PAIR

        def body(l, carry):
            up_w = W[l, :, :, :, 0:F].reshape(D, F)
            down_w = W[l, :, :, :, F:W3].reshape(D, H)
            gate = Gs[l, r0:r1, 0:1]
            projected = dot(Xs[l, r0:r1], up_w, (1, 0))
            g, u = projected[:, :H], projected[:, H:]
            s = jax.nn.sigmoid(g)
            gs = g * s
            hidden = (gs * u * gate).astype(BF16)
            GH[l, r0:r1] = hidden
            d_hidden = dot(Cs[l, r0:r1], down_w, (1, 0)) * gate
            d_gate = d_hidden * u * s * (1.0 + g * (1.0 - s))
            d_proj = jnp.concatenate([d_gate, d_hidden * gs], axis=1).astype(BF16)
            DP[l, r0:r1] = d_proj
            return carry

        lax.fori_loop(l0, l1, body, 0)

    def outer(i0, i1):
        r0, r1 = i0 * PAIR, i1 * PAIR

        def body(l, carry):
            out = dot(GH[l, r0:r1], W[l, :, :, :, F:W3].reshape(D, H), (1, 1)).astype(BF16)
            back = dot(DP[l, r0:r1], W[l, :, :, :, 0:F].reshape(D, F), (1, 1)).astype(BF16)
            at = pl.ds(pl.multiple_of(l * PAIR, 16), PAIR)
            for i in range(i0, i1):
                part = slice((i - i0) * PAIR, (i - i0 + 1) * PAIR)
                OR[i, at, :] = out[part]
                GR[i, at, :] = back[part]
            return carry

        lax.fori_loop(0, L, body, 0)

    def combine(i0, i1):
        def body(i, carry):
            picked = Pm[i]
            xg[i] = dot(picked, OR[i], (0, 0)).astype(BF16)
            cg[i] = dot(picked, GR[i], (0, 0)).astype(BF16)
            return carry

        for i in range(i0, i1):
            for copy in reading.pop(i, []):
                copy.wait_send()
        lax.fori_loop(i0, i1, body, 0)
        for i in range(i0, i1):
            send(xg.at[i, pl.ds(TOK, TOK)], sibo.at[i], rsib_s.at[0, i], rsib_r.at[0, i], sib)
            send(cg.at[i, pl.ds(TOK, TOK)], sibg.at[i], rsib_s.at[1, i], rsib_r.at[1, i], sib)

    EARLY = 5 * PAIR

    def own(l):
        return Q.at[l // 2] if l % 2 == 0 else W.at[l]

    def early(l):
        own(l)[:, :, :, 0:F] = dot(Xs[l, 0:EARLY], DP[l, 0:EARLY], (0, 0)).astype(BF16).reshape(NX, NX, 64, F)
        own(l)[:, :, :, F:W3] = dot(Cs[l, 0:EARLY], GH[l, 0:EARLY], (0, 0)).astype(BF16).reshape(NX, NX, 64, H)

    def gradient(l):
        for slots, units, first, last in ((Xs, DP, 0, F), (Cs, GH, F, W3)):
            start = EARLY if l % 2 == 0 else 0
            term = dot(slots[l, start:SLOTS], units[l, start:SLOTS], (0, 0)).reshape(NX, NX, 64, last - first)
            if l % 2 == 0:
                term = term + own(l)[:, :, :, first:last].astype(F32)
            own(l)[:, :, :, first:last] = term.astype(BF16)

    def gradient_piece(l, q):
        columns = pl.ds(pl.multiple_of(q * 256, 256), 256)
        for slots, units, first, last in ((Xs, DP, 0, F), (Cs, GH, F, W3)):
            term = dot(slots[l, EARLY:SLOTS, columns], units[l, EARLY:SLOTS], (0, 0)).reshape(NX, 64, last - first)
            own(l)[q, :, :, first:last] = (term + own(l)[q, :, :, first:last].astype(F32)).astype(BF16)

    for group in range(NX):
        relayout(group)
    for copy in own_copies:
        copy.wait()
    hop(1, (2, 0))
    hop(1, (1,))
    for distance in (0, 1, 7):
        dispatch(distance)
    hop(2, (2, 0))
    hop(2, (1,))
    dispatch(2)
    dispatch(6)
    inner(0, 5)
    outer(0, 5)
    hop(3, (2, 0))
    early(0)
    early(2)
    hop(3, (1,))
    combine(0, 5)
    dispatch(3)
    dispatch(5)
    hop(4, (2, 0, 1))
    dispatch(4)

    def chunk(h, q, n):
        return (n, q) if h == 0 else (q, n)

    def axes(h, stage):
        along_x = (h == 0) == (stage == 1)
        return (xx, xp, xm) if along_x else (yy, yp, ym)

    def second(h, o):
        return (axes(h, 2)[0] + o) % NX

    def far1(h, way, o):
        at, plus, minus = axes(h, 1)
        n = second(h, o)
        send(
            own(2 * h + way).at[chunk(h, (at + 2) % NX, n)], fwd1.at[h, way, n],
            x1_s.at[h, way, o], x1_r.at[h, way, o], (plus, minus)[way],
        )

    def near1(h, way):
        at, plus, minus = axes(h, 1)
        l, q = 2 * h + 1 - way, (at + (1, 3)[way]) % NX
        source = own(l).at[:, q] if h == 0 else own(l).at[q]
        send(source, fin1.at[h, way, 1 - way], x1_s.at[h, way, 4], x1_r.at[h, way, 4], (plus, minus)[way])

    def relay1(h, way, o):
        at, plus, minus = axes(h, 1)
        n = second(h, o)
        arrived(fwd1.at[h, way, n], x1_r.at[h, way, o])
        mine = own(2 * h + way)[chunk(h, (at + (1, 3)[way]) % NX, n)]
        fwd1[h, way, n] = (fwd1[h, way, n].astype(F32) + mine.astype(F32)).astype(BF16)
        send(
            fwd1.at[h, way, n], fin1.at[h, way, way, n],
            x1_s.at[h, way, 5 + o], x1_r.at[h, way, 5 + o], (plus, minus)[way],
        )

    def settle1(h, o):
        at = axes(h, 1)[0]
        n = second(h, o)
        for way in range(2):
            if o == 2:
                arrived(fin1.at[h, way, 1 - way], x1_r.at[h, way, 4])
            arrived(fin1.at[h, way, way, n], x1_r.at[h, way, 5 + o])
        for slot in range(2):
            held_ref, index = own(2 * h + slot), chunk(h, at, n)
            total = held_ref[index].astype(F32) + fin1[h, 0, slot, n].astype(F32) + fin1[h, 1, slot, n].astype(F32)
            held_ref[index] = total.astype(BF16)

    def held(h, l, q):
        return own(l).at[chunk(h, axes(h, 1)[0], q)]

    def far2(h):
        for way in range(2):
            send(
                held(h, 2 * h + way, second(h, 2)), fwd2.at[h, way],
                x2_s.at[h, way, 0], x2_r.at[h, way, 0], axes(h, 2)[1 + way],
            )

    def near2(h, way):
        send(
            held(h, 2 * h + 1 - way, second(h, (1, 3)[way])), fin2.at[h, way, 1 - way],
            x2_s.at[h, way, 1], x2_r.at[h, way, 1], axes(h, 2)[1 + way],
        )

    def relay2(h, way):
        arrived(fwd2.at[h, way], x2_r.at[h, way, 0])
        mine = held(h, 2 * h + way, second(h, (1, 3)[way]))[...]
        fwd2[h, way] = (fwd2[h, way].astype(F32) + mine.astype(F32)).astype(BF16)
        send(fwd2.at[h, way], fin2.at[h, way, way], x2_s.at[h, way, 2], x2_r.at[h, way, 2], axes(h, 2)[1 + way])

    def settle2(h):
        for way in range(2):
            arrived(fin2.at[h, way, 1 - way], x2_r.at[h, way, 1])
            arrived(fin2.at[h, way, way], x2_r.at[h, way, 2])
        for slot in range(2):
            l = 2 * h + slot
            total = own(l)[yy, xx].astype(F32) + fin2[h, 0, slot].astype(F32) + fin2[h, 1, slot].astype(F32)
            fs[l] = total.astype(BF16)

    def total_of(parts):
        total = parts[0].astype(F32)
        for part in parts[1:]:
            total = total + part.astype(F32)
        return total.astype(BF16)

    ways = (
        (0, 0, (4, 3, 2, 1), rlp, zp),
        (1, 1, (4, 5, 6, 7), rgm, zm),
        (1, 0, (3, 2, 1), rgp, zp),
        (0, 1, (5, 6, 7), rlm, zm),
    )

    HALF = TOK // 2

    def reduce_step(j, part):
        rows = slice(part * HALF, (part + 1) * HALF)
        span = pl.ds(part * HALF, HALF)
        for t, way, targets, slots, peer in ways:
            if j >= len(targets):
                continue
            i = place(targets[j])
            mine, other = ((xg, sibo), (cg, sibg))[t]
            if part == 0:
                arrived(other.at[i], rsib_r.at[t, i])
            parts = [mine[i, rows, :], other[i, rows, :]]
            if j > 0:
                arrived(slots.at[j - 1, span], rz_r.at[t, way, j - 1, part])
                parts.append(slots[j - 1, rows, :])
            mine[i, rows, :] = total_of(parts)
            send(mine.at[i, span], slots.at[j, span], rz_s.at[t, way, j, part], rz_r.at[t, way, j, part], peer)

    def reduce_end(part):
        i = place(0)
        rows = slice(part * HALF, (part + 1) * HALF)
        span = pl.ds(part * HALF, HALF)
        for t, mine, other, plus, minus, out in ((0, xg, sibo, rlp, rlm, lo_ref), (1, cg, sibg, rgp, rgm, go_ref)):
            np_, nm = (3, 2) if t == 0 else (2, 3)
            if part == 0:
                arrived(other.at[i], rsib_r.at[t, i])
            arrived(plus.at[np_, span], rz_r.at[t, 0, np_, part])
            arrived(minus.at[nm, span], rz_r.at[t, 1, nm, part])
            out[rows, :] = total_of([mine[i, rows, :], other[i, rows, :], plus[np_, rows, :], minus[nm, rows, :]])

    inner(5, 8, 0, 1)
    gradient(0)
    for o in (2, 1, 3, 0):
        far1(0, 0, o)
    near1(0, 1)
    inner(5, 8, 2, 3)
    gradient_piece(2, (yy + 2) % NX)
    for o in (2, 1, 3, 0):
        far1(1, 0, o)
    gradient_piece(2, (yy + 3) % NX)
    near1(1, 1)
    inner(5, 8, 1, 2)
    inner(5, 8, 3, 4)
    outer(5, 8)
    combine(7, 8)
    combine(5, 7)
    reduce_step(0, 0)
    reduce_step(0, 1)
    gradient(1)
    for o in (2, 1, 3, 0):
        far1(0, 1, o)
    near1(0, 0)
    gradient(3)
    for o in (2, 1, 3, 0):
        far1(1, 1, o)
    near1(1, 0)
    gradient_piece(2, (yy + 1) % NX)
    gradient_piece(2, yy)
    for h in range(2):
        for o in (2, 1, 3, 0):
            relay1(h, 0, o)
    reduce_step(1, 0)
    for h in range(2):
        relay1(h, 1, 2)
    reduce_step(1, 1)
    for o in (1, 3):
        for h in range(2):
            relay1(h, 1, o)
    reduce_step(2, 0)
    for h in range(2):
        relay1(h, 1, 0)
    for h in range(2):
        settle1(h, 2)
        far2(h)
    reduce_step(2, 1)
    for o, way in ((1, 0), (3, 1)):
        for h in range(2):
            settle1(h, o)
            near2(h, way)
    reduce_step(3, 0)
    for h in range(2):
        settle1(h, 0)
    for h in range(2):
        for way in range(2):
            relay2(h, way)
    reduce_step(3, 1)
    reduce_end(0)
    settle2(0)
    settle2(1)
    reduce_end(1)
    ogu_ref[...] = jnp.swapaxes(fs[:, :, 0:F], 0, 1)
    odn_ref[...] = jnp.swapaxes(fs[:, :, F:W3], 0, 1)
    for copy in sends:
        copy.wait_send()


def move(*refs):
    for n in range(4):
        refs[4 + n][...] = refs[n][...]


def per_device(tokens, routes, gate_weights, cotangent, w_gate_up, w_down):
    vmem = pl.BlockSpec(memory_space=pltpu.VMEM)
    hbm = pl.BlockSpec(memory_space=pl.ANY)
    dma = pltpu.SemaphoreType.DMA
    rows = D // (NX * NX)
    results = pl.pallas_call(
        kernel,
        out_shape=(
            jax.ShapeDtypeStruct((TOK, D), BF16),
            jax.ShapeDtypeStruct((TOK, D), BF16),
            jax.ShapeDtypeStruct((rows, L, F), BF16),
            jax.ShapeDtypeStruct((rows, L, H), BF16),
        ),
        in_specs=[hbm, vmem, vmem, hbm, hbm, hbm],
        out_specs=(vmem, vmem, vmem, vmem),
        scratch_shapes=[
            pltpu.VMEM((L, NX, NX, rows, W3), BF16),
            pltpu.VMEM((2, NX, NX, rows, W3), BF16),
            pltpu.VMEM((256, L, F), BF16),
            pltpu.VMEM((256, L, H), BF16),
            pltpu.VMEM((NZ, 2 * TOK, D), BF16),
            pltpu.VMEM((NZ, 2 * TOK, D), BF16),
            pltpu.VMEM((NZ, 2, 16, TOK), F32),
            pltpu.VMEM((L, SLOTS, D), BF16),
            pltpu.VMEM((L, SLOTS, D), BF16),
            pltpu.VMEM((L, SLOTS, H), BF16),
            pltpu.VMEM((L, SLOTS, F), BF16),
            pltpu.VMEM((L, SLOTS, TOK), F32),
            pltpu.VMEM((NZ, ROWS, 2 * TOK), BF16),
            pltpu.VMEM((NZ, ROWS, D), BF16),
            pltpu.VMEM((NZ, ROWS, D), BF16),
            pltpu.VMEM((NZ, TOK, D), BF16),
            pltpu.VMEM((NZ, TOK, D), BF16),
            pltpu.VMEM((4, TOK, D), BF16),
            pltpu.VMEM((3, TOK, D), BF16),
            pltpu.VMEM((3, TOK, D), BF16),
            pltpu.VMEM((4, TOK, D), BF16),
            pltpu.VMEM((2, 2, NX, rows, W3), BF16),
            pltpu.VMEM((2, 2, 2, NX, rows, W3), BF16),
            pltpu.VMEM((2, 2, rows, W3), BF16),
            pltpu.VMEM((2, 2, 2, rows, W3), BF16),
            pltpu.VMEM((L, rows, W3), BF16),
            dma((3, 2, 4)), dma((3, NZ)), dma((3, NZ)), dma((3, NZ)),
            dma((2, NZ)), dma((2, NZ)), dma((2, 2, 4, 2)), dma((2, 2, 4, 2)),
            dma((2, 2, 9)), dma((2, 2, 9)), dma((2, 2, 3)), dma((2, 2, 3)),
            dma((2,)), dma((2,)),
        ],
        compiler_params=pltpu.CompilerParams(
            collective_id=0, has_side_effects=True, vmem_limit_bytes=63 << 20
        ),
    )(tokens, routes.T, gate_weights.T, cotangent, w_gate_up, w_down)
    return pl.pallas_call(
        move,
        out_shape=tuple(jax.ShapeDtypeStruct(a.shape, a.dtype) for a in results),
        in_specs=[vmem] * 4,
        out_specs=(vmem,) * 4,
    )(*results)


def solution(mesh):
    rows = P(("dp", "expert"), None)
    return jax.shard_map(
        per_device,
        mesh=mesh,
        in_specs=(rows, rows, rows, rows, P(None, "expert", None), P(None, "expert", None)),
        out_specs=(rows, rows, P("dp", "expert", None), P("dp", "expert", None)),
        check_vma=False,
    )
```
